256 devices in a mesh: batch: 16 (over x, y_hi, core), seq: 16 (over z, y_lo).
Axes of the slice: x: 4, y: 4 (y_hi: 2, y_lo: 2; y = y_hi * 2 + y_lo), z: 8, core: 2. Of those that a mesh axis runs over, the one named last changes fastest.
Arguments:
- dna_features: bfloat16 [131072, 768], P(('batch', 'seq')), parts along dimension 0, may hold values from -6 to 6
- conv_weight: bfloat16 [5, 768, 1536], P(None, None, 'seq'), may hold values from -0.09375 to 0.09375
- conv_bias: float32 [1536], replicated, may hold values from -3 to 3
- norm_gain: float32 [1536], replicated, may hold values from 0.5 to 1.5
- qkv_weight: bfloat16 [3, 1536, 768], P(None, None, 'seq'), may hold values from -0.15625 to 0.15625
- head_scale: float32 [4], replicated, may hold values from 1.5 to 60, as said below
- out_weight: bfloat16 [768, 1536], P(None, 'seq'), may hold values from -0.21875 to 0.21875
Outputs:
- block_out: bfloat16 [65536, 1536], P(('batch', 'seq')), parts along dimension 0
The draws below stay inside these ranges and needn't reach their ends.
There are 16 independent parts, one for each index of `batch`. The reference program is written for one: setup_inputs(seed, part) draws one part's arguments, and reference() takes and returns one part's arrays. A program takes and returns all parts, laid end to end along the dimension named above; an argument that names none is the same for every part. Nothing has to cross between parts.
Inputs may be any that keep to these rules, and one draw needn't show every extreme that they name: `head_scale`: one positive factor per head.
All inputs are finite; a program needn't handle non-finite values.
Results may differ from the reference program's by a relative error of at most 0.017.
The reference program's roundings to bfloat16 on the way count: a program that leaves them out, or rounds other values in their place, can miss the bound.
Values may be sent and summed in bfloat16 or wider, within the bound.
No kernel may reach another device: no remote copies, remote signals or barrier semaphores. Data moves between devices by JAX's collectives and lax.ppermute only.
A program may use at most 128 MiB of HBM per device.

```python
import math
import jax
import jax.numpy as jnp
from jax import lax

C = 1536
CIN = 768
TAPS = 5
HEADS = 4
HEAD_DIM = 192
POSITIONS = 8192


def draw_head_scale(key, part):
    return jnp.exp(jax.random.uniform(key, (HEADS,), jnp.float32, math.log(1.5), math.log(4.0)))


def shard_levels(rng, extent, pieces, smallest, high):
    def one(axis_at, blocks):
        draws = jax.random.uniform(jax.random.fold_in(jax.random.fold_in(rng, 6), axis_at), (blocks,), jnp.float32, smallest / len(pieces), high / len(pieces))
        return jnp.repeat(jnp.exp(draws), extent[axis_at] // blocks).reshape((-1,) + (1,) * (len(extent) - axis_at - 1))

    factor_of = one(*pieces[0])
    for cut in pieces[1:]:
        factor_of = factor_of * one(*cut)
    return factor_of


def gaussian(key, extent, scale, bound, shards=(), kind=jnp.bfloat16):
    loudness = shard_levels(key, extent, shards, -0.22, 0.18) if shards else 1.0
    result = jax.random.normal(key, extent, jnp.float32) * scale * loudness
    return jnp.minimum(jnp.maximum(result, -bound), bound).astype(kind)


def setup_inputs(seed: int = 0, part: int = 0) -> dict:
    streams_of = jax.random.split(jax.random.key(seed), 8)
    part_splits = jax.random.split(jax.random.fold_in(streams_of[7], part), 8)
    dna_features = gaussian(part_splits[0], (POSITIONS, CIN), 1.0, 6.0, ((0, 16),))
    conv_weight = gaussian(streams_of[1], (TAPS, CIN, C), (TAPS * CIN) ** -0.5, 0.09375, ((2, 16),))
    conv_bias = gaussian(streams_of[2], (C,), 0.5, 3.0, (), jnp.float32)
    norm_gain = jnp.clip(1.0 + 0.1 * jax.random.normal(streams_of[3], (C,), jnp.float32), 0.5, 1.5)
    qkv_weight = gaussian(streams_of[4], (3, C, HEADS * HEAD_DIM), C ** -0.5, 0.15625, ((2, 16),))
    head_scale = draw_head_scale(jax.random.fold_in(streams_of[7], 71), part)
    out_weight = gaussian(streams_of[6], (HEADS * HEAD_DIM, C), (HEADS * HEAD_DIM) ** -0.5, 0.21875, ((1, 16),))
    return dict(dna_features=dna_features, conv_weight=conv_weight, conv_bias=conv_bias, norm_gain=norm_gain, qkv_weight=qkv_weight, head_scale=head_scale, out_weight=out_weight)


def reference(dna_features, conv_weight, conv_bias, norm_gain, qkv_weight, head_scale, out_weight):
    activated = jax.nn.gelu(dna_features.astype(jnp.float32), approximate=True).astype(jnp.bfloat16)
    half_taps = TAPS // 2
    positions = activated.shape[0]
    padded = jnp.pad(activated, ((half_taps, half_taps), (0, 0)))
    summed = jnp.zeros((positions, C), jnp.float32) + conv_bias
    for tap in range(TAPS):
        summed = summed + jnp.dot(padded[tap:tap + positions], conv_weight[tap], preferred_element_type=jnp.float32)
    pooled = lax.optimization_barrier(jnp.max(summed.reshape(positions // 2, 2, C), axis=1)).astype(jnp.bfloat16)
    values32 = pooled.astype(jnp.float32)
    centre = lax.optimization_barrier(jnp.mean(values32, axis=1, keepdims=True))
    spread = lax.optimization_barrier(jnp.mean((values32 - centre) ** 2, axis=1, keepdims=True))
    normed = ((values32 - centre) * lax.rsqrt(spread + 1e-05) * norm_gain).astype(jnp.bfloat16)
    queries = jnp.dot(normed, qkv_weight[0], preferred_element_type=jnp.float32).astype(jnp.bfloat16)
    keys = jnp.dot(normed, qkv_weight[1], preferred_element_type=jnp.float32).astype(jnp.bfloat16)
    values = jnp.dot(normed, qkv_weight[2], preferred_element_type=jnp.float32).astype(jnp.bfloat16)
    tokens = queries.shape[0]
    head_q = queries.reshape(tokens, HEADS, HEAD_DIM).transpose(1, 0, 2)
    head_k = keys.reshape(tokens, HEADS, HEAD_DIM).transpose(1, 0, 2)
    head_v = values.reshape(tokens, HEADS, HEAD_DIM).transpose(1, 0, 2)
    factor = head_scale / math.sqrt(HEAD_DIM)

    def one_head(items):
        query_h, key_h, value_h, factor_h = items
        scores = jnp.dot(query_h, key_h.T, preferred_element_type=jnp.float32) * factor_h
        top = lax.optimization_barrier(jnp.max(scores, axis=1, keepdims=True))
        weights = jnp.exp(scores - top)
        denom = lax.optimization_barrier(jnp.sum(weights, axis=1, keepdims=True))
        return jnp.dot(weights.astype(jnp.bfloat16), value_h, preferred_element_type=jnp.float32) / denom
    heads_out = lax.map(one_head, (head_q, head_k, head_v, factor))
    attended = heads_out.transpose(1, 0, 2).reshape(tokens, HEADS * HEAD_DIM).astype(jnp.bfloat16)
    mixed = jnp.dot(attended, out_weight, preferred_element_type=jnp.float32)
    return (pooled.astype(jnp.float32) + mixed).astype(jnp.bfloat16)
```

```python
import functools
import math

import jax
import jax.numpy as jnp
from jax import lax
from jax.experimental import pallas as pl
from jax.experimental.pallas import tpu as pltpu
from jax.sharding import PartitionSpec as P

HEADS = 4
HEAD_DIM = 192
AXES = ("batch", "seq")
F32 = jnp.float32
BF16 = jnp.bfloat16
DELTAS = (0, 1, -1, 2)
VMEM_BYTES = 60 * 1024 * 1024


def place(index):
    low, z = index % 2, (index // 2) % 8
    core, high, x = (index // 16) % 2, (index // 32) % 2, index // 64
    return x, 2 * high + low, z, core


def flat(x, y, z, core):
    x, y, z = x % 4, y % 4, z % 8
    return (((x * 2 + y // 2) * 2 + core) * 8 + z) * 2 + y % 2


def send(value, target):
    pairs = [(i, flat(*target(*place(i)))) for i in range(256)]
    return lax.ppermute(value, AXES, pairs)


def spread_z(x, y, z, core):
    return x, y, (z - x) % 4 + 4 * core, z // 4


def first(step):
    return lambda x, y, z, core: (x + step, y, z, core) if core == 0 else (x, y + step, z, core)


def second(step):
    return lambda x, y, z, core: (x, y + step, z, core) if core == 0 else (x + step, y, z, core)


def other_core(x, y, z, core):
    return x, y, z, 1 - core


def other_low(x, y, z, core):
    return x, y ^ 1, z, core


def gather_plane(block):
    block = send(block, spread_z)
    one = [block, send(block, first(1)), send(block, first(-1)), send(block, first(2))]
    stack = jnp.stack(one)
    low, high = send(stack, second(1)), send(stack, second(-1))
    far_a = send(low[:2], second(1))
    far_b = send(high[2:], second(-1))
    return (stack, low, high, far_a, far_b), (
        [(a, 0) for a in range(4)],
        [(a, 1) for a in range(4)],
        [(a, 2) for a in range(4)],
        [(0, 3), (1, 3)],
        [(2, 3), (3, 3)],
    )


def slot_rows(slots, x, y, z, core):
    rows = []
    for group in slots:
        for a, b in group:
            along, across = DELTAS[a], DELTAS[b]
            px = jnp.where(core == 0, x - along, x - across) % 4
            py = jnp.where(core == 0, y - across, y - along) % 4
            rows.append(((px + z) % 4) * 4 + (py % 2) * 2 + py // 2)
    return jnp.stack(rows).astype(jnp.int32)


def nt(a, b):
    return lax.dot_general(a, b, (((1,), (1,)), ((), ())), preferred_element_type=F32)


def conv_kernel(rows, acts, bias, g0, g1, g2, g3, g4, out, weights, sems):
    at = 0
    copies = [[] for _ in range(5)]
    for group in (g0, g1, g2, g3, g4):
        for slot in range(group.shape[0]):
            for tap in range(5):
                copy = pltpu.make_async_copy(
                    group.at[slot, tap], weights.at[tap, rows[at]], sems.at[tap, at]
                )
                copy.start()
                copies[tap].append(copy)
            at += 1
    for tap in range(5):
        for copy in copies[tap]:
            copy.wait()
    for block in range(3):
        even = odd = None
        for tap in range(5):
            w = weights[tap].reshape(768, 768)[256 * block : 256 * block + 256]
            e, o = nt(acts[tap], w), nt(acts[tap + 1], w)
            even = e if even is None else even + e
            odd = o if odd is None else odd + o
        lanes = slice(256 * block, 256 * block + 256)
        out[:, lanes] = (jnp.maximum(even, odd) + bias[:, lanes]).astype(BF16)


def project_kernel(meta, mine, theirs, gain, g0, g1, g2, g3, g4, b0, b1, b2, b3, weights, normed, sems):
    at = 0
    copies = []
    for group in (g0, g1, g2, g3, g4):
        for slot in range(group.shape[0]):
            row = meta[at]
            copy = pltpu.make_async_copy(
                group.at[slot, pl.ds(0, 3)], weights.at[:, row % 2, row // 2], sems.at[at]
            )
            copy.start()
            copies.append(copy)
            at += 1
    core = meta[16]
    for part in range(2):
        here = mine[pl.ds(256 * part, 256), :].astype(F32)
        there = theirs[pl.ds(256 * (1 - part), 256), :].astype(F32)
        total = jnp.sum(here, axis=1, keepdims=True) + jnp.sum(there, axis=1, keepdims=True)
        centre = total / 1536.0
        here, there = here - centre, there - centre
        spread = (
            jnp.sum(here * here, axis=1, keepdims=True)
            + jnp.sum(there * there, axis=1, keepdims=True)
        ) / 1536.0
        rate = lax.rsqrt(spread + 1e-05)
        normed[part, core] = (here * rate * gain[core]).astype(BF16)
        normed[part, 1 - core] = (there * rate * gain[1 - core]).astype(BF16)
    for copy in copies:
        copy.wait()
    for number, block in enumerate((b0, b1, b2, b3)):
        part, head = meta[17 + 2 * number], meta[18 + 2 * number]
        low, high = normed[part, 0], normed[part, 1]
        for j in range(3):
            w0 = weights[j, 0, pl.ds(4 * head, 4)].reshape(192, 768)
            w1 = weights[j, 1, pl.ds(4 * head, 4)].reshape(192, 768)
            block[j] = (nt(w0, low) + nt(w1, high)).astype(BF16)


def attend_kernel(factor, own, near, far, far_near, out, scores):
    scale = factor[0]
    groups = (own, near, far, far_near)

    def one(part, _):
        query = own[part, 2].T
        top = None
        for at in range(16):
            key = groups[at // 4][at % 4, 0]
            s = jnp.dot(query, key, preferred_element_type=F32) * scale
            scores[at] = s
            top = s if top is None else jnp.maximum(top, s)
        top = jnp.max(top, axis=1, keepdims=True)
        total = acc = None
        for at in range(16):
            p = jnp.exp(scores[at] - top)
            total = p if total is None else total + p
            o = nt(p.astype(BF16), groups[at // 4][at % 4, 1])
            acc = o if acc is None else acc + o
        out[part] = (acc / jnp.sum(total, axis=1, keepdims=True)).astype(BF16).T
        return 0

    lax.fori_loop(0, 4, one, 0)


def out_kernel(meta, h0, h1, h2, h3, mine, theirs, *refs):
    groups, other, out, weights, attended, sems = refs[:5], refs[5:10], *refs[10:]
    core = meta[16]
    copies = []
    for side, (base, which) in enumerate(((groups, core), (other, 1 - core))):
        at = 0
        for group in base:
            for slot in range(group.shape[0]):
                source = group.at[slot, 3] if side == 0 else group.at[slot]
                copy = pltpu.make_async_copy(
                    source, weights.at[which, meta[17 * side + at]], sems.at[side, at]
                )
                copy.start()
                copies.append(copy)
                at += 1
    for number, head in enumerate((h0, h1, h2, h3)):
        attended[meta[33 + number]] = head[...].T
    for copy in copies:
        copy.wait()
    heads = [attended[h] for h in range(4)]
    left = jnp.where(core == 0, mine[pl.ds(0, 256), :], theirs[pl.ds(256, 256), :])
    right = jnp.where(core == 0, theirs[pl.ds(256, 256), :], mine[pl.ds(0, 256), :])
    rows = jnp.concatenate(heads, axis=1)
    for half, base in enumerate((left, right)):
        w = weights[half].reshape(768, 768)
        out[:, 768 * half : 768 * half + 768] = (base.astype(F32) + nt(rows, w)).astype(BF16)


SMEM = pl.BlockSpec(memory_space=pltpu.SMEM)
VMEM = pl.BlockSpec(memory_space=pltpu.VMEM)
ANY = pl.BlockSpec(memory_space=pl.ANY)


def call(kernel, ins, outs, scratch, flops, *args):
    return pl.pallas_call(
        kernel,
        out_shape=outs,
        in_specs=ins,
        out_specs=jax.tree.map(lambda _: VMEM, outs),
        scratch_shapes=scratch,
        compiler_params=pltpu.CompilerParams(vmem_limit_bytes=VMEM_BYTES),
        cost_estimate=pl.CostEstimate(flops=flops, bytes_accessed=8_000_000, transcendentals=0),
    )(*args)


def shards(dna_features, conv_weight, conv_bias, norm_gain, qkv_weight, head_scale, out_weight):
    batch, seq = lax.axis_index("batch"), lax.axis_index("seq")
    x, high, core = batch // 4, (batch // 2) % 2, batch % 2
    z, low = seq // 2, seq % 2
    y = 2 * high + low

    taps = lax.dynamic_slice_in_dim(conv_weight.transpose(0, 2, 1), 48 * high, 48, axis=1)
    qkv = lax.dynamic_slice_in_dim(qkv_weight.transpose(0, 2, 1), 768 * high, 768, axis=2)
    last = lax.dynamic_slice_in_dim(out_weight.T, 48 * high, 48, axis=0)
    order = jnp.stack([qkv[1], qkv[2], qkv[0], last])
    conv_groups, slots = gather_plane(taps)
    groups, _ = gather_plane(order)
    rows = slot_rows(slots, x, y, z, core)

    activated = jax.nn.gelu(dna_features.astype(F32), approximate=True).astype(BF16)
    forward = [(16 * b + i, 16 * b + i + 1) for b in range(16) for i in range(15)]
    backward = [(t, s) for s, t in forward]
    before = lax.ppermute(activated[-2:], AXES, forward)
    after = lax.ppermute(activated[:2], AXES, backward)
    padded = jnp.concatenate([before, activated, after], axis=0).reshape(258, 2, 768)
    pairs = jnp.stack([padded[:, 0], padded[:, 1]])
    both = [pairs, send(pairs, other_core)]
    acts = jnp.stack(
        [
            jnp.concatenate([w[i % 2, i // 2 : i // 2 + 256] for w in both], axis=0)
            for i in range(6)
        ]
    )
    bias = lax.dynamic_slice_in_dim(conv_bias, 768 * core, 768).reshape(1, 768)
    mine = call(
        conv_kernel,
        [SMEM, VMEM, VMEM] + [ANY] * 5,
        jax.ShapeDtypeStruct((512, 768), BF16),
        [pltpu.VMEM((5, 16, 48, 768), BF16), pltpu.SemaphoreType.DMA((5, 16))],
        6_000_000_000,
        rows,
        acts,
        bias,
        *conv_groups,
    )
    theirs = send(mine, other_core)

    sends = []
    for m in range(4):
        sends.append((z // 2 + m) % 4)
    meta = [rows, core.reshape(1)]
    for index in sends:
        window, head = index % 2, index // 2
        meta.append(jnp.stack([jnp.where(window == core, 0, 1), head]))
    meta = jnp.concatenate([v.astype(jnp.int32) for v in meta])
    blocks = call(
        project_kernel,
        [SMEM, VMEM, VMEM, VMEM] + [ANY] * 5,
        [jax.ShapeDtypeStruct((3, 192, 256), BF16)] * 4,
        [
            pltpu.VMEM((3, 2, 8, 48, 768), BF16),
            pltpu.VMEM((2, 2, 256, 768), BF16),
            pltpu.SemaphoreType.DMA((16,)),
        ],
        1_800_000_000,
        meta,
        mine,
        theirs,
        norm_gain.reshape(2, 1, 768),
        *groups,
    )
    own = [
        send(
            block,
            lambda x, y, z, core, m=m: (x, y, 2 * ((z // 2 + m) % 4) + core, z % 2),
        )
        for m, block in enumerate(blocks)
    ]
    own = jnp.stack(own)
    kv = own[:, :2]
    near = send(kv, other_core)
    far = send(kv, other_low)
    far_near = send(far, other_core)
    factor = head_scale / math.sqrt(HEAD_DIM)
    mine_factor = lax.dynamic_slice_in_dim(factor, 2 * (z % 2) + z // 4, 1)
    heads = call(
        attend_kernel,
        [SMEM] + [VMEM] * 4,
        jax.ShapeDtypeStruct((4, 192, 256), BF16),
        [pltpu.VMEM((16, 256, 256), F32)],
        3_200_000_000,
        mine_factor,
        own,
        near,
        far,
        far_near,
    )
    back = []
    for n in range(4):
        h = 2 * (z % 2) + z // 4
        m = (z // 2 - (h + n)) % 4
        block = lax.dynamic_index_in_dim(heads, m, 0, keepdims=False)
        back.append(
            send(
                block,
                lambda x, y, z, core, n=n: (
                    x,
                    y,
                    2 * ((2 * (z % 2) + z // 4 + n) % 4) + core,
                    (z // 2) % 2,
                ),
            )
        )
    from_heads = [(z // 2 - n) % 4 for n in range(4)]
    other_rows = slot_rows(slots, x, y, z, 1 - core)
    others = [send(g[:, 3], other_core) for g in groups]
    meta = jnp.concatenate(
        [rows, core.reshape(1).astype(jnp.int32), other_rows, jnp.stack(from_heads).astype(jnp.int32)]
    )
    return call(
        out_kernel,
        [SMEM] + [VMEM] * 6 + [ANY] * 10,
        jax.ShapeDtypeStruct((256, 1536), BF16),
        [
            pltpu.VMEM((2, 16, 48, 768), BF16),
            pltpu.VMEM((4, 256, 192), BF16),
            pltpu.SemaphoreType.DMA((2, 16)),
        ],
        600_000_000,
        meta,
        *back,
        mine,
        theirs,
        *groups,
        *others,
    )


def solution(mesh):
    placed = (
        P(AXES, None),
        P(None, None, "seq"),
        P(),
        P(),
        P(None, None, "seq"),
        P(),
        P(None, "seq"),
    )
    return jax.shard_map(
        shards, mesh=mesh, in_specs=placed, out_specs=P(AXES, None), check_vma=False
    )
```

```python
import math

import jax
import jax.numpy as jnp
import numpy as np
from jax import lax
from jax.experimental import pallas as pl
from jax.experimental.pallas import tpu as pltpu
from jax.sharding import PartitionSpec as P

HEADS = 4
HEAD_DIM = 192
AXES = ("batch", "seq")
F32 = jnp.float32
BF16 = jnp.bfloat16
DELTAS = (0, 1, -1, 2)
SLOTS = [(a, b) for b in range(4) for a in range(4)]
BYTES = 8_000_000
VMEM_BYTES = 60 * 1024 * 1024


def place(index):
    low, z = index % 2, (index // 2) % 8
    core, high, x = (index // 16) % 2, (index // 32) % 2, index // 64
    return x, 2 * high + low, z, core


def flat(x, y, z, core):
    x, y, z = x % 4, y % 4, z % 8
    return (((x * 2 + y // 2) * 2 + core) * 8 + z) * 2 + y % 2


def send(value, target, name):
    pairs = [(i, flat(*target(*place(i)))) for i in range(256)]
    with jax.named_scope(name):
        return lax.ppermute(value, AXES, pairs)


SPREAD = {
    (0, 0): ((3, 1, 0, 2), (0, 2, 1, 3), (2, 0, 3, 1), (1, 3, 2, 0)),
    (0, 1): ((2, 3, 0, 1), (0, 2, 1, 3), (3, 1, 2, 0), (1, 0, 3, 2)),
    (1, 0): ((1, 0, 3, 2), (0, 2, 1, 3), (3, 1, 2, 0), (2, 3, 0, 1)),
    (1, 1): ((2, 1, 3, 0), (0, 2, 1, 3), (3, 0, 2, 1), (1, 3, 0, 2)),
}


def origin_z(x, z, core):
    return SPREAD[core, z // 4][x % 4][z % 4]


def spread_z(x, y, z, core):
    (target,) = [i for i in range(4) if origin_z(x, 4 * core + i, z // 4) == z % 4]
    return x, y, 4 * core + target, z // 4


def first(step):
    return lambda x, y, z, core: (x + step, y, z, core) if core == 0 else (x, y + step, z, core)


def second(step):
    return lambda x, y, z, core: (x, y + step, z, core) if core == 0 else (x + step, y, z, core)


def other_core(x, y, z, core):
    return x, y, z, 1 - core


def other_low(x, y, z, core):
    return x, y ^ 1, z, core


def after(value, *others):
    zero = sum((o[(0,) * o.ndim].astype(F32) * 0.0 for o in others), F32(0.0))
    return value + zero.astype(value.dtype)


def stacked(blocks):
    out = jnp.zeros((len(blocks), *blocks[0].shape), blocks[0].dtype)
    for at, block in enumerate(blocks):
        out = lax.dynamic_update_slice(out, block[None], (at,) + (0,) * block.ndim)
    return out


def gather_first(block):
    return [block] + [send(block, first(step), "weights_first") for step in (1, -1, 2)]


ROWS, CORE, SENDS, HEAD, STEPS, OTHER, FROM = 0, 16, 17, 25, 26, 30, 46


def slot_rows(x, y, z, core):
    rows = []
    for a, b in SLOTS:
        along, across = (DELTAS[a], DELTAS[b]) if core == 0 else (DELTAS[b], DELTAS[a])
        px, py = (x - along) % 4, (y - across) % 4
        rows.append(origin_z(px, z, core) * 4 + (py % 2) * 2 + py // 2)
    return rows


def shift(m, core, parity):
    return (2, -2, 0, 4)[m] + core - parity


def to_head(m):
    return lambda x, y, z, core: (x, y, (z + shift(m, core, z % 2)) % 8, z % 2)


BACK = {
    (0, 0): ((1, 2, 3, 0), (3, 0, 1, 2), (0, 3, 2, 1), (2, 1, 0, 3)),
    (0, 1): ((2, 3, 0, 1), (0, 1, 2, 3), (1, 2, 3, 0), (3, 0, 1, 2)),
    (1, 0): ((0, 1, 3, 2), (3, 2, 1, 0), (2, 3, 0, 1), (1, 0, 2, 3)),
    (1, 1): ((2, 3, 0, 1), (0, 1, 2, 3), (3, 0, 1, 2), (1, 2, 3, 0)),
}


def back_z(n, z, core):
    return 2 * BACK[(z // 2) % 2, core][n][2 * (z // 4) + z % 2] + core


def to_tokens(n):
    return lambda x, y, z, core: (x, y, back_z(n, z, core), (z // 2) % 2)


def integers(index):
    x, y, z, core = place(index)
    row = slot_rows(x, y, z, core) + [core]
    for m in range(4):
        target = (z + shift(m, core, z % 2)) % 8
        row += [0 if (target // 2) % 2 == core else 1, target // 4]
    row.append(2 * (z % 2) + z // 4)
    source = {(z - shift(m, z % 2, core)) % 8: m for m in range(4)}
    row += [source[back_z(n, z, core)] for n in range(4)]
    row += slot_rows(x, y, z, 1 - core)
    for n in range(4):
        (origin,) = [
            a for a in range(8) if (a // 2) % 2 == core and back_z(n, a, z % 2) == z
        ]
        row.append(2 * (origin % 2) + origin // 4)
    return row


TABLE = np.array([integers(i) for i in range(256)], np.int32)


def nt(a, b):
    return lax.dot_general(a, b, (((1,), (1,)), ((), ())), preferred_element_type=F32)


def acts_kernel(own, other, out):
    for which, window in enumerate((own, other)):
        for odd in range(2):
            row = lax.broadcasted_iota(jnp.int32, (272, 528), 0)
            col = lax.broadcasted_iota(jnp.int32, (272, 528), 1)
            pick = jnp.where(col == 2 * row + odd, 1.0, 0.0).astype(BF16)
            rows = jnp.dot(pick, window[...], preferred_element_type=F32)
            for step in range(3):
                out[2 * step + odd, pl.ds(256 * which, 256), :] = rows[step : step + 256].astype(BF16)


def conv_kernel(base, table, acts, bias, *refs):
    *groups, out, weights, sems = refs
    groups = groups[-3:] if base == 0 else groups[-2:]
    copies = [[] for _ in range(5)]
    for tap in range(5):
        at = 0
        for group in groups:
            for slot in range(group.shape[0]):
                copy = pltpu.make_async_copy(
                    group.at[slot, tap], weights.at[tap, at], sems.at[tap, at]
                )
                copy.start()
                copies[tap].append(copy)
                at += 1
    for tap in range(5):
        for copy in copies[tap]:
            copy.wait()

    def block(number, _):
        even = odd = None
        for tap in range(5):
            w = weights[tap, pl.ds(4 * number, 4)].reshape(192, 768)
            e, o = nt(acts[tap], w), nt(acts[tap + 1], w)
            even = e if even is None else even + e
            odd = o if odd is None else odd + o
        at = base + 4 * number
        shift = jnp.concatenate([bias[table[ROWS + at + i]] for i in range(4)], axis=1)
        pooled = (jnp.maximum(even, odd) + shift).T.astype(BF16)
        out[pl.ds(4 * number, 4)] = pooled.reshape(4, 48, 512)
        return 0

    lax.fori_loop(0, weights.shape[1] // 4, block, 0)


def project_kernel(table, ma, mb, ta, tb, gain, g0, g1, g2, g3, g4, out, last, tokens, weights, normed, sems):
    at = 0
    copies = []
    for group in (g0, g1, g2, g3, g4):
        for slot in range(group.shape[0]):
            row = table[ROWS + at]
            for source, target in (
                (group.at[slot, pl.ds(0, 3)], weights.at[:, row % 2, row // 2]),
                (group.at[slot, 3], last.at[row]),
            ):
                copy = pltpu.make_async_copy(source, target, sems.at[len(copies)])
                copy.start()
                copies.append(copy)
            at += 1
    core = table[CORE]
    for at in range(16):
        a, b = (ma, at) if at < 12 else (mb, at - 12)
        tokens[core, table[ROWS + at]] = a[b]
        a = ta if at < 12 else tb
        row = table[OTHER + at]
        tokens[1 - core, row, :, :256] = a[b, :, 256:]
        tokens[1 - core, row, :, 256:] = a[b, :, :256]

    def norm(part, _):
        cols = pl.ds(pl.multiple_of(256 * part, 256), 256)
        values = [tokens[half, :, :, cols].astype(F32).reshape(768, 256) for half in range(2)]
        centre = sum(jnp.sum(v, axis=0, keepdims=True) for v in values) / 1536.0
        values = [v - centre for v in values]
        spread = sum(jnp.sum(v * v, axis=0, keepdims=True) for v in values) / 1536.0
        rate = lax.rsqrt(spread + 1e-05)
        for half in range(2):
            normed[part, half] = (values[half] * rate * gain[half]).astype(BF16)
        return 0

    lax.fori_loop(0, 2, norm, 0)
    for copy in copies:
        copy.wait()

    def one(m, _):
        part, head = table[SENDS + 2 * m], table[SENDS + 1 + 2 * m]
        total = None
        for half in range(2):
            w = weights[:, half, pl.ds(4 * head, 4)].reshape(576, 768)
            term = jnp.dot(w, normed[part, half], preferred_element_type=F32)
            total = term if total is None else total + term
        out[m] = total.astype(BF16).reshape(3, 192, 256)
        return 0

    lax.fori_loop(0, 4, one, 0)


def scores_of(query, groups, scores, scale):
    top = None
    for at, group in enumerate(groups):
        keys = jnp.concatenate([group[i, 0] for i in range(group.shape[0])], axis=1)
        s = jnp.dot(query, keys, preferred_element_type=F32) * scale
        scores[at, :, : s.shape[1]] = s
        t = jnp.max(s, axis=1, keepdims=True)
        top = t if top is None else jnp.maximum(top, t)
    return top


def sums_of(top, groups, scores):
    total = acc = None
    for at, group in enumerate(groups):
        values = jnp.concatenate([group[i, 1] for i in range(group.shape[0])], axis=1)
        p = jnp.exp(scores[at, :, : values.shape[1]] - top)
        t = jnp.sum(p, axis=1, keepdims=True)
        o = nt(p.astype(BF16), values)
        total = t if total is None else total + t
        acc = o if acc is None else acc + o
    return total, acc


def attend_kernel(table, factor, queries, g0, g1, g2, g3, tops, totals, accs, scores):
    scale = factor[table[HEAD]] * (1 / math.sqrt(HEAD_DIM))

    def one(part, _):
        groups = (g0, g1, g2, g3)
        top = scores_of(queries[part].T, groups, scores, scale)
        total, acc = sums_of(top, groups, scores)
        tops[part] = jnp.broadcast_to(top, (256, 128))
        totals[part] = jnp.broadcast_to(total, (256, 128))
        accs[part] = acc
        return 0

    lax.fori_loop(0, 4, one, 0)


def finish_kernel(base, table, factor, *refs):
    queries, g0, g1, g2, g3, tops, totals, accs, out, scores = refs[-10:]
    scale = factor[table[HEAD]] * (1 / math.sqrt(HEAD_DIM))

    def one(step, _):
        part = table[STEPS + base[0] + step]
        groups = (g0, g1, g2, g3)
        before = tops[part, :, :1]
        top = jnp.maximum(before, scores_of(queries[part].T, groups, scores, scale))
        total, acc = sums_of(top, groups, scores)
        keep = jnp.exp(before - top)
        total = total + totals[part, :, :1] * keep
        acc = acc + accs[part] * keep
        out[step] = (acc / total).astype(BF16).T
        return 0

    lax.fori_loop(0, 2, one, 0)


def base_kernel(tokens, out):
    for half in range(2):
        out[:, 768 * half : 768 * half + 768] = tokens[half, :, :, :256].reshape(768, 256).T


def out_kernel(table, h0, h1, h2, h3, base, mine, theirs, out, weights, attended, sems):
    core = table[CORE]
    copies = []
    for side, (group, which) in enumerate(((mine, core), (theirs, 1 - core))):
        copy = pltpu.make_async_copy(group, weights.at[which], sems.at[side])
        copy.start()
        copies.append(copy)
    for number, head in enumerate((h0, h1, h2, h3)):
        attended[table[FROM + number]] = head[...].T
    rows = jnp.concatenate([attended[h] for h in range(4)], axis=1)
    for copy in copies:
        copy.wait()
    for half in range(2):
        lanes = slice(768 * half, 768 * half + 768)
        w = weights[half].reshape(768, 768)
        out[:, lanes] = (base[:, lanes].astype(F32) + nt(rows, w)).astype(BF16)


SMEM = pl.BlockSpec(memory_space=pltpu.SMEM)
VMEM = pl.BlockSpec(memory_space=pltpu.VMEM)
ANY = pl.BlockSpec(memory_space=pl.ANY)


def call(kernel, ins, outs, scratch, flops, *args):
    kernel_name = getattr(kernel, '__name__', 'kernel').replace('<lambda>', 'conv_kernel')
    return pl.pallas_call(
        kernel,
        out_shape=outs,
        in_specs=ins,
        out_specs=jax.tree.map(lambda _: VMEM, outs),
        scratch_shapes=scratch,
        compiler_params=pltpu.CompilerParams(vmem_limit_bytes=VMEM_BYTES),
        cost_estimate=pl.CostEstimate(flops=flops, bytes_accessed=BYTES, transcendentals=0),
        name=kernel_name,
    )(*args)


def shape(*dims, dtype=BF16):
    return jax.ShapeDtypeStruct(dims, dtype)


def shards(dna_features, conv_weight, conv_bias, norm_gain, qkv_weight, head_scale, out_weight):
    batch, seq = lax.axis_index("batch"), lax.axis_index("seq")
    core, high = batch % 2, (batch // 2) % 2
    table = lax.dynamic_index_in_dim(TABLE, batch * 16 + seq, 0, keepdims=False)

    taps = lax.dynamic_slice_in_dim(conv_weight.transpose(0, 2, 1), 48 * high, 48, axis=1)
    qkv = lax.dynamic_slice_in_dim(qkv_weight.transpose(0, 2, 1), 768 * high, 768, axis=2)
    last = lax.dynamic_slice_in_dim(out_weight.T, 48 * high, 48, axis=0)
    block = jnp.concatenate([taps, qkv[1:], qkv[:1], last[None]], axis=0)
    features = after(dna_features, block)
    block = send(block, spread_z, "weights_z")

    activated = jax.nn.gelu(features.astype(F32), approximate=True).astype(BF16)
    forward = [(16 * b + i, 16 * b + i + 1) for b in range(16) for i in range(15)]
    backward = [(t, s) for s, t in forward]
    before = lax.ppermute(activated[-2:], AXES, forward)
    behind = lax.ppermute(activated[:2], AXES, backward)
    padded = jnp.concatenate([before, activated, behind, jnp.zeros((12, 768), BF16)], axis=0)
    acts = call(
        acts_kernel,
        [VMEM] * 2,
        shape(6, 512, 768),
        [],
        1_000_000_000,
        padded,
        send(padded, other_core, "acts_core"),
    )

    pieces = gather_first(block)
    stack = stacked([after(pieces[0][:5], acts)] + [p[:5] for p in pieces[1:]])
    low, high_stack = [send(stack, second(step), "conv_second") for step in (1, -1)]
    far = (
        send(low[:2], second(1), "conv_far"),
        send(high_stack[2:], second(-1), "conv_far"),
    )
    qkv_stack = stacked([after(pieces[0][5:], low, high_stack)] + [p[5:] for p in pieces[1:]])
    qkv_near = [send(qkv_stack, second(step), "qkv_second") for step in (1, -1)]
    qkv_groups = (
        qkv_stack,
        *qkv_near,
        send(qkv_near[0][:2], second(1), "qkv_far"),
        send(qkv_near[1][2:], second(-1), "qkv_far"),
    )
    bias = lax.dynamic_slice_in_dim(conv_bias, 768 * core, 768).reshape(16, 1, 48)

    def conv(base, groups, *earlier):
        count = sum(g.shape[0] for g in groups)
        return call(
            lambda *refs: conv_kernel(base, *refs),
            [SMEM, VMEM, VMEM] + [ANY] * (len(groups) + len(earlier)),
            shape(count, 48, 512),
            [pltpu.VMEM((5, count, 48, 768), BF16), pltpu.SemaphoreType.DMA((5, count))],
            375_000_000 * count,
            table,
            acts,
            bias,
            *earlier,
            *groups,
        )

    mine = [conv(0, (stack, low, high_stack))]
    mine.append(conv(12, far, mine[0]))
    theirs = [send(m, other_core, "pooled_core") for m in mine]
    blocks, last, tokens = call(
        project_kernel,
        [SMEM] + [VMEM] * 5 + [ANY] * 5,
        [shape(4, 3, 192, 256), shape(16, 48, 768), shape(2, 16, 48, 512)],
        [
            pltpu.VMEM((3, 2, 8, 48, 768), BF16),
            pltpu.VMEM((2, 2, 768, 256), BF16),
            pltpu.SemaphoreType.DMA((32,)),
        ],
        1_800_000_000,
        table,
        *mine,
        *theirs,
        norm_gain.reshape(2, 768, 1),
        *qkv_groups,
    )

    own = [send(blocks[m], to_head(m), "qkv_z") for m in range(2)]
    later = after(blocks, *own)
    first_keys = jnp.stack([o[:2] for o in own])
    own += [send(later[m], to_head(m), "qkv_z_later") for m in range(2, 4)]
    second_keys = jnp.stack([o[:2] for o in own[2:]])
    queries = jnp.stack([o[2] for o in own])

    def shared(keys, *earlier):
        far = send(keys, other_low, "keys_y")
        return keys, send(keys, other_core, "keys_core"), far, send(after(far, *earlier), other_core, "keys_y_core")

    partial = call(
        attend_kernel,
        [SMEM, SMEM] + [VMEM] * 5,
        [
            shape(4, 256, 128, dtype=F32),
            shape(4, 256, 128, dtype=F32),
            shape(4, 256, 192, dtype=F32),
        ],
        [pltpu.VMEM((4, 256, 512), F32)],
        1_600_000_000,
        table,
        head_scale,
        queries,
        *shared(first_keys),
    )
    base = call(base_kernel, [VMEM], shape(256, 1536), [], 1_000_000, tokens)
    other_last = send(after(last, queries), other_core, "out_core")
    late = (queries, *shared(second_keys, partial[0]), *partial)
    heads = []
    for number in range(2):
        heads.append(
            call(
                finish_kernel,
                [SMEM, SMEM, SMEM] + [VMEM] * (8 + number),
                shape(2, 192, 256),
                [pltpu.VMEM((4, 256, 512), F32)],
                800_000_000,
                jnp.full((1,), 2 * number, jnp.int32),
                table,
                head_scale,
                *heads,
                *late,
            )
        )
    back = [send(heads[n // 2][n % 2], to_tokens(n), "heads_back") for n in range(4)]
    return call(
        out_kernel,
        [SMEM] + [VMEM] * 5 + [ANY] * 2,
        shape(256, 1536),
        [
            pltpu.VMEM((2, 16, 48, 768), BF16),
            pltpu.VMEM((4, 256, 192), BF16),
            pltpu.SemaphoreType.DMA((2,)),
        ],
        600_000_000,
        table,
        *back,
        base,
        last,
        other_last,
    )


def solution(mesh):
    placed = (
        P(AXES, None),
        P(None, None, "seq"),
        P(),
        P(),
        P(None, None, "seq"),
        P(),
        P(None, "seq"),
    )
    return jax.shard_map(
        shards, mesh=mesh, in_specs=placed, out_specs=P(AXES, None), check_vma=False
    )
```

```python
import math

import jax
import jax.numpy as jnp
import numpy as np
from jax import lax
from jax.experimental import pallas as pl
from jax.experimental.pallas import tpu as pltpu
from jax.sharding import PartitionSpec as P

HEADS = 4
HEAD_DIM = 192
AXES = ("batch", "seq")
F32 = jnp.float32
BF16 = jnp.bfloat16
DELTAS = (0, 1, -1, 2)
SLOTS = [(a, b) for b in range(4) for a in range(4)]
BYTES = 8_000_000
VMEM_BYTES = 60 * 1024 * 1024


def place(index):
    low, z = index % 2, (index // 2) % 8
    core, high, x = (index // 16) % 2, (index // 32) % 2, index // 64
    return x, 2 * high + low, z, core


def flat(x, y, z, core):
    x, y, z = x % 4, y % 4, z % 8
    return (((x * 2 + y // 2) * 2 + core) * 8 + z) * 2 + y % 2


def send(value, target, name):
    pairs = [(i, flat(*target(*place(i)))) for i in range(256)]
    with jax.named_scope(name):
        return lax.ppermute(value, AXES, pairs)


SPREAD = {
    (0, 0): ((3, 1, 0, 2), (0, 2, 1, 3), (2, 0, 3, 1), (1, 3, 2, 0)),
    (0, 1): ((2, 3, 0, 1), (0, 2, 1, 3), (3, 1, 2, 0), (1, 0, 3, 2)),
    (1, 0): ((1, 0, 3, 2), (0, 2, 1, 3), (3, 1, 2, 0), (2, 3, 0, 1)),
    (1, 1): ((2, 1, 3, 0), (0, 2, 1, 3), (3, 0, 2, 1), (1, 3, 0, 2)),
}


def origin_z(x, z, core):
    return SPREAD[core, z // 4][x % 4][z % 4]


def spread_z(x, y, z, core):
    (target,) = [i for i in range(4) if origin_z(x, 4 * core + i, z // 4) == z % 4]
    return x, y, 4 * core + target, z // 4


def first(step):
    return lambda x, y, z, core: (x + step, y, z, core) if core == 0 else (x, y + step, z, core)


def second(step):
    return lambda x, y, z, core: (x, y + step, z, core) if core == 0 else (x + step, y, z, core)


def other_core(x, y, z, core):
    return x, y, z, 1 - core


def other_low(x, y, z, core):
    return x, y ^ 1, z, core


def after(value, *others):
    zero = sum((o[(0,) * o.ndim].astype(F32) * 0.0 for o in others), F32(0.0))
    return value + zero.astype(value.dtype)


def stacked(blocks):
    out = jnp.zeros((len(blocks), *blocks[0].shape), blocks[0].dtype)
    for at in reversed(range(len(blocks))):
        out = lax.dynamic_update_slice(out, blocks[at][None], (at,) + (0,) * blocks[at].ndim)
    return out


def gather_first(block):
    return [block] + [send(block, first(step), "weights_first") for step in (1, -1, 2)]


ROWS, CORE, SENDS, HEAD, STEPS, OTHER, FROM = 0, 16, 17, 25, 26, 30, 46


def slot_rows(x, y, z, core):
    rows = []
    for a, b in SLOTS:
        along, across = (DELTAS[a], DELTAS[b]) if core == 0 else (DELTAS[b], DELTAS[a])
        px, py = (x - along) % 4, (y - across) % 4
        rows.append(origin_z(px, z, core) * 4 + (py % 2) * 2 + py // 2)
    return rows


def shift(m, core, parity):
    return (2, -2, 0, 4)[m] + core - parity


def to_head(m):
    return lambda x, y, z, core: (x, y, (z + shift(m, core, z % 2)) % 8, z % 2)


BACK = {
    (0, 0): ((1, 2, 3, 0), (3, 0, 1, 2), (0, 3, 2, 1), (2, 1, 0, 3)),
    (0, 1): ((2, 3, 0, 1), (0, 1, 2, 3), (1, 2, 3, 0), (3, 0, 1, 2)),
    (1, 0): ((0, 1, 3, 2), (3, 2, 1, 0), (2, 3, 0, 1), (1, 0, 2, 3)),
    (1, 1): ((2, 3, 0, 1), (0, 1, 2, 3), (3, 0, 1, 2), (1, 2, 3, 0)),
}


def back_z(n, z, core):
    return 2 * BACK[(z // 2) % 2, core][n][2 * (z // 4) + z % 2] + core


def to_tokens(n):
    return lambda x, y, z, core: (x, y, back_z(n, z, core), (z // 2) % 2)


def integers(index):
    x, y, z, core = place(index)
    row = slot_rows(x, y, z, core) + [core]
    for m in range(4):
        target = (z + shift(m, core, z % 2)) % 8
        row += [0 if (target // 2) % 2 == core else 1, target // 4]
    row.append(2 * (z % 2) + z // 4)
    source = {(z - shift(m, z % 2, core)) % 8: m for m in range(4)}
    row += [source[back_z(n, z, core)] for n in range(4)]
    row += slot_rows(x, y, z, 1 - core)
    for n in range(4):
        (origin,) = [
            a for a in range(8) if (a // 2) % 2 == core and back_z(n, a, z % 2) == z
        ]
        row.append(2 * (origin % 2) + origin // 4)
    return row


TABLE = np.array([integers(i) for i in range(256)], np.int32)


def nt(a, b):
    return lax.dot_general(a, b, (((1,), (1,)), ((), ())), preferred_element_type=F32)


def acts_kernel(own, other, out):
    for which, window in enumerate((own, other)):
        columns = window[...].T

        def one(number, _):
            row = lax.broadcasted_iota(jnp.int32, (528, 256), 0)
            col = lax.broadcasted_iota(jnp.int32, (528, 256), 1)
            pick = jnp.where(row == 2 * col + number, 1.0, 0.0).astype(BF16)
            picked = jnp.dot(columns, pick, preferred_element_type=F32)
            out[number, :, 256 * which : 256 * which + 256] = picked.astype(BF16)
            return 0

        lax.fori_loop(0, 6, one, 0)


def conv_kernel(base, table, acts, bias, *refs):
    *groups, out, weights, sems = refs
    groups = groups[-3:] if base == 0 else groups[-2:]
    copies = []
    at = 0
    for group in groups:
        for slot in range(group.shape[0]):
            for tap in range(5):
                copy = pltpu.make_async_copy(
                    group.at[slot, tap],
                    weights.at[at, :, pl.ds(768 * tap, 768)],
                    sems.at[at, tap],
                )
                copy.start()
                copies.append(copy)
            at += 1
    count = at
    shift = jnp.concatenate([bias[table[ROWS + base + i]] for i in range(count)], axis=0)
    for copy in copies:
        copy.wait()

    def block(number, _):
        cols = pl.ds(pl.multiple_of(256 * number, 256), 256)
        w = weights[...].reshape(48 * count, 3840)
        even = jnp.dot(w, acts[0:5, :, cols].reshape(3840, 256), preferred_element_type=F32)
        odd = jnp.dot(w, acts[1:6, :, cols].reshape(3840, 256), preferred_element_type=F32)
        pooled = (jnp.maximum(even, odd) + shift).astype(BF16)
        out[:, :, cols] = pooled.reshape(count, 48, 256)
        return 0

    lax.fori_loop(0, 2, block, 0)


def project_kernel(table, ma, mb, ta, tb, gain, g0, g1, g2, g3, g4, out, query, last, tokens, weights, normed, sems):
    at = 0
    copies = []
    for group in (g0, g1, g2, g3, g4):
        for slot in range(group.shape[0]):
            row = table[ROWS + at]
            for source, target in (
                (group.at[slot, pl.ds(0, 3)], weights.at[:, row % 2, row // 2]),
                (group.at[slot, 3], last.at[row]),
            ):
                copy = pltpu.make_async_copy(source, target, sems.at[len(copies)])
                copy.start()
                copies.append(copy)
            at += 1
    core = table[CORE]
    for at in range(16):
        a, b = (ma, at) if at < 12 else (mb, at - 12)
        tokens[core, table[ROWS + at]] = a[b]
        a = ta if at < 12 else tb
        row = table[OTHER + at]
        tokens[1 - core, row, :, :256] = a[b, :, 256:]
        tokens[1 - core, row, :, 256:] = a[b, :, :256]

    def norm(part, _):
        cols = pl.ds(pl.multiple_of(256 * part, 256), 256)
        values = [tokens[half, :, :, cols].astype(F32).reshape(768, 256) for half in range(2)]
        centre = sum(jnp.sum(v, axis=0, keepdims=True) for v in values) / 1536.0
        values = [v - centre for v in values]
        spread = sum(jnp.sum(v * v, axis=0, keepdims=True) for v in values) / 1536.0
        rate = lax.rsqrt(spread + 1e-05)
        for half in range(2):
            normed[part, half] = (values[half] * rate * gain[half]).astype(BF16)
        return 0

    lax.fori_loop(0, 2, norm, 0)
    for copy in copies:
        copy.wait()

    def one(m, _):
        part, head = table[SENDS + 2 * m], table[SENDS + 1 + 2 * m]
        total = None
        for half in range(2):
            w = weights[:, half, pl.ds(4 * head, 4)].reshape(576, 768)
            term = jnp.dot(w, normed[part, half], preferred_element_type=F32)
            total = term if total is None else total + term
        out[m] = total[:384].astype(BF16).reshape(2, 192, 256)
        query[m] = total[384:].astype(BF16)
        return 0

    lax.fori_loop(0, 4, one, 0)


def scores_of(query, groups, scores):
    top = None
    for at, group in enumerate(groups):
        keys = jnp.concatenate([group[i, 0] for i in range(group.shape[0])], axis=1)
        s = jnp.dot(query, keys, preferred_element_type=F32)
        scores[at, :, : s.shape[1]] = s
        t = jnp.max(s, axis=1, keepdims=True)
        top = t if top is None else jnp.maximum(top, t)
    return top


def sums_of(top, groups, scores, scale):
    top = top * scale
    total = acc = None
    for at, group in enumerate(groups):
        values = jnp.concatenate([group[i, 1] for i in range(group.shape[0])], axis=1)
        p = jnp.exp2(scores[at, :, : values.shape[1]] * scale - top)
        t = jnp.sum(p, axis=1, keepdims=True)
        o = nt(p.astype(BF16), values)
        total = t if total is None else total + t
        acc = o if acc is None else acc + o
    return total, acc


def attend_kernel(table, factor, queries, g0, g1, tops, totals, accs, scores):
    scale = factor[table[HEAD]] * (math.log2(math.e) / math.sqrt(HEAD_DIM))

    def one(part, _):
        groups = (g0, g1)
        top = scores_of(queries[part].T, groups, scores)
        total, acc = sums_of(top, groups, scores, scale)
        tops[part] = jnp.broadcast_to(top, (256, 128))
        totals[part] = jnp.broadcast_to(total, (256, 128))
        accs[part] = acc
        return 0

    lax.fori_loop(0, 4, one, 0)


def finish_kernel(table, factor, queries, g0, g1, tops, totals, accs, out, scores):
    scale = factor[table[HEAD]] * (math.log2(math.e) / math.sqrt(HEAD_DIM))

    def one(step, _):
        part = table[STEPS + step]
        groups = (g0, g1)
        before = tops[part, :, :1]
        top = jnp.maximum(before, scores_of(queries[part].T, groups, scores))
        total, acc = sums_of(top, groups, scores, scale)
        keep = jnp.exp2((before - top) * scale)
        total = total + totals[part, :, :1] * keep
        acc = acc + accs[part] * keep
        out[step] = (acc / total).astype(BF16).T
        return 0

    lax.fori_loop(0, 4, one, 0)


def base_kernel(tokens, out):
    for half in range(2):
        out[:, 768 * half : 768 * half + 768] = tokens[half, :, :, :256].reshape(768, 256).T


def out_kernel(table, h0, h1, h2, h3, base, mine, theirs, out, attended):
    core = table[CORE]
    for number, head in enumerate((h0, h1, h2, h3)):
        attended[table[FROM + number]] = head[...]
    rows = attended[...].reshape(768, 256).T
    for which, weights in ((core, mine), (1 - core, theirs)):
        lanes = pl.ds(pl.multiple_of(768 * which, 768), 768)
        mixed = nt(rows, weights[...].reshape(768, 768))
        out[:, lanes] = (base[:, lanes].astype(F32) + mixed).astype(BF16)


SMEM = pl.BlockSpec(memory_space=pltpu.SMEM)
VMEM = pl.BlockSpec(memory_space=pltpu.VMEM)
ANY = pl.BlockSpec(memory_space=pl.ANY)


def call(kernel, ins, outs, scratch, flops, *args):
    kernel_name = getattr(kernel, '__name__', 'kernel').replace('<lambda>', 'conv_kernel')
    return pl.pallas_call(
        kernel,
        out_shape=outs,
        in_specs=ins,
        out_specs=jax.tree.map(lambda _: VMEM, outs),
        scratch_shapes=scratch,
        compiler_params=pltpu.CompilerParams(vmem_limit_bytes=VMEM_BYTES),
        cost_estimate=pl.CostEstimate(flops=flops, bytes_accessed=BYTES, transcendentals=0),
        name=kernel_name,
    )(*args)


def shape(*dims, dtype=BF16):
    return jax.ShapeDtypeStruct(dims, dtype)


def shards(dna_features, conv_weight, conv_bias, norm_gain, qkv_weight, head_scale, out_weight):
    batch, seq = lax.axis_index("batch"), lax.axis_index("seq")
    core, high = batch % 2, (batch // 2) % 2
    table = lax.dynamic_index_in_dim(TABLE, batch * 16 + seq, 0, keepdims=False)

    taps = lax.dynamic_slice_in_dim(conv_weight.transpose(0, 2, 1), 48 * high, 48, axis=1)
    qkv = lax.dynamic_slice_in_dim(qkv_weight.transpose(0, 2, 1), 768 * high, 768, axis=2)
    last = lax.dynamic_slice_in_dim(out_weight.T, 48 * high, 48, axis=0)
    block = jnp.concatenate([taps, qkv[1:], qkv[:1], last[None]], axis=0)
    features = after(dna_features, block)
    block = send(block, spread_z, "weights_z")

    activated = jax.nn.gelu(features.astype(F32), approximate=True).astype(BF16)
    forward = [(16 * b + i, 16 * b + i + 1) for b in range(16) for i in range(15)]
    backward = [(t, s) for s, t in forward]
    before = lax.ppermute(activated[-2:], AXES, forward)
    behind = lax.ppermute(activated[:2], AXES, backward)
    padded = jnp.concatenate([before, activated, behind, jnp.zeros((12, 768), BF16)], axis=0)
    acts = call(
        acts_kernel,
        [VMEM] * 2,
        shape(6, 768, 512),
        [],
        1_000_000_000,
        padded,
        send(padded, other_core, "acts_core"),
    )

    pieces = gather_first(block)
    stack = stacked([after(pieces[0][:5], acts)] + [p[:5] for p in pieces[1:]])
    low, high_stack = [send(stack, second(step), "conv_second") for step in (1, -1)]
    far = (
        send(low[:2], second(1), "conv_far"),
        send(high_stack[2:], second(-1), "conv_far"),
    )
    qkv_stack = stacked([after(pieces[0][5:], low, high_stack)] + [p[5:] for p in pieces[1:]])
    qkv_near = [send(qkv_stack, second(step), "qkv_second") for step in (1, -1)]
    qkv_groups = (
        qkv_stack,
        *qkv_near,
        send(qkv_near[0][:2], second(1), "qkv_far"),
        send(qkv_near[1][2:], second(-1), "qkv_far"),
    )
    bias = lax.dynamic_slice_in_dim(conv_bias, 768 * core, 768).reshape(16, 48, 1)

    def conv(base, groups, *earlier):
        count = sum(g.shape[0] for g in groups)
        return call(
            lambda *refs: conv_kernel(base, *refs),
            [SMEM, VMEM, VMEM] + [ANY] * (len(groups) + len(earlier)),
            shape(count, 48, 512),
            [pltpu.VMEM((count, 48, 3840), BF16), pltpu.SemaphoreType.DMA((count, 5))],
            375_000_000 * count,
            table,
            acts,
            bias,
            *earlier,
            *groups,
        )

    mine = [conv(0, (stack, low, high_stack))]
    mine.append(conv(12, far, mine[0]))
    theirs = [send(m, other_core, "pooled_core") for m in mine]
    blocks, query, last, tokens = call(
        project_kernel,
        [SMEM] + [VMEM] * 5 + [ANY] * 5,
        [
            shape(4, 2, 192, 256),
            shape(4, 192, 256),
            shape(16, 48, 768),
            shape(2, 16, 48, 512),
        ],
        [
            pltpu.VMEM((3, 2, 8, 48, 768), BF16),
            pltpu.VMEM((2, 2, 768, 256), BF16),
            pltpu.SemaphoreType.DMA((32,)),
        ],
        1_800_000_000,
        table,
        *mine,
        *theirs,
        norm_gain.reshape(2, 768, 1),
        *qkv_groups,
    )

    keys = jnp.stack([send(blocks[m], to_head(m), "keys_z") for m in range(4)])
    far = send(keys, other_low, "keys_y")
    near = send(keys, other_core, "keys_core")
    query = after(query, keys)
    queries = jnp.stack([send(query[m], to_head(m), "queries_z") for m in range(4)])

    partial = call(
        attend_kernel,
        [SMEM, SMEM] + [VMEM] * 3,
        [
            shape(4, 256, 128, dtype=F32),
            shape(4, 256, 128, dtype=F32),
            shape(4, 256, 192, dtype=F32),
        ],
        [pltpu.VMEM((2, 256, 1024), F32)],
        1_600_000_000,
        table,
        head_scale,
        queries,
        keys,
        near,
    )
    base = call(base_kernel, [VMEM], shape(256, 1536), [], 1_000_000, tokens)
    other_last = send(after(last, queries), other_core, "out_core")
    far_near = send(after(far, partial[0]), other_core, "keys_y_core")
    heads = call(
        finish_kernel,
        [SMEM, SMEM] + [VMEM] * 6,
        shape(4, 192, 256),
        [pltpu.VMEM((2, 256, 1024), F32)],
        1_600_000_000,
        table,
        head_scale,
        queries,
        far,
        far_near,
        *partial,
    )
    back = [send(heads[n], to_tokens(n), "heads_back") for n in range(4)]
    return call(
        out_kernel,
        [SMEM] + [VMEM] * 7,
        shape(256, 1536),
        [pltpu.VMEM((4, 192, 256), BF16)],
        600_000_000,
        table,
        *back,
        base,
        last,
        other_last,
    )


def solution(mesh):
    placed = (
        P(AXES, None),
        P(None, None, "seq"),
        P(),
        P(),
        P(None, None, "seq"),
        P(),
        P(None, "seq"),
    )
    return jax.shard_map(
        shards, mesh=mesh, in_specs=placed, out_specs=P(AXES, None), check_vma=False
    )
```

```python
import math

import jax
import jax.numpy as jnp
import numpy as np
from jax import lax
from jax.experimental import pallas as pl
from jax.experimental.pallas import tpu as pltpu
from jax.sharding import PartitionSpec as P

HEADS = 4
HEAD_DIM = 192
AXES = ("batch", "seq")
F32 = jnp.float32
BF16 = jnp.bfloat16
DELTAS = (0, 1, -1, 2)
SLOTS = [(a, b) for b in range(4) for a in range(4)]
BYTES = 8_000_000
VMEM_BYTES = 60 * 1024 * 1024


def place(index):
    low, z = index % 2, (index // 2) % 8
    core, high, x = (index // 16) % 2, (index // 32) % 2, index // 64
    return x, 2 * high + low, z, core


def flat(x, y, z, core):
    x, y, z = x % 4, y % 4, z % 8
    return (((x * 2 + y // 2) * 2 + core) * 8 + z) * 2 + y % 2


def send(value, target, name):
    pairs = [(i, flat(*target(*place(i)))) for i in range(256)]
    with jax.named_scope(name):
        return lax.ppermute(value, AXES, pairs)


SPREAD = {
    (0, 0): ((3, 1, 0, 2), (0, 2, 1, 3), (2, 0, 3, 1), (1, 3, 2, 0)),
    (0, 1): ((2, 3, 0, 1), (0, 2, 1, 3), (3, 1, 2, 0), (1, 0, 3, 2)),
    (1, 0): ((1, 0, 3, 2), (0, 2, 1, 3), (3, 1, 2, 0), (2, 3, 0, 1)),
    (1, 1): ((2, 1, 3, 0), (0, 2, 1, 3), (3, 0, 2, 1), (1, 3, 0, 2)),
}


def origin_z(x, z, core):
    return SPREAD[core, z // 4][x % 4][z % 4]


def spread_z(x, y, z, core):
    (target,) = [i for i in range(4) if origin_z(x, 4 * core + i, z // 4) == z % 4]
    return x, y, 4 * core + target, z // 4


def first(step):
    return lambda x, y, z, core: (x + step, y, z, core) if core == 0 else (x, y + step, z, core)


def second(step):
    return lambda x, y, z, core: (x, y + step, z, core) if core == 0 else (x + step, y, z, core)


def other_core(x, y, z, core):
    return x, y, z, 1 - core


def other_low(x, y, z, core):
    return x, y ^ 1, z, core


def after(value, *others):
    zero = sum((o[(0,) * o.ndim].astype(F32) * 0.0 for o in others), F32(0.0))
    return value + zero.astype(value.dtype)


def stacked(blocks):
    out = jnp.zeros((len(blocks), *blocks[0].shape), blocks[0].dtype)
    for at in reversed(range(len(blocks))):
        out = lax.dynamic_update_slice(out, blocks[at][None], (at,) + (0,) * blocks[at].ndim)
    return out


def gather_first(block, name):
    return [block] + [send(block, first(step), name) for step in (1, -1, 2)]


ROWS, CORE, SENDS, HEAD, STEPS, OTHER, FROM = 0, 16, 17, 25, 26, 30, 46


def slot_rows(x, y, z, core):
    rows = []
    for a, b in SLOTS:
        along, across = (DELTAS[a], DELTAS[b]) if core == 0 else (DELTAS[b], DELTAS[a])
        px, py = (x - along) % 4, (y - across) % 4
        rows.append(origin_z(px, z, core) * 4 + (py % 2) * 2 + py // 2)
    return rows


def shift(m, core, parity):
    return (2, -2, 0, 4)[m] + core - parity


def to_head(m):
    return lambda x, y, z, core: (x, y, (z + shift(m, core, z % 2)) % 8, z % 2)


BACK = {
    (0, 0): ((1, 2, 3, 0), (3, 0, 1, 2), (0, 3, 2, 1), (2, 1, 0, 3)),
    (0, 1): ((2, 3, 0, 1), (0, 1, 2, 3), (1, 2, 3, 0), (3, 0, 1, 2)),
    (1, 0): ((0, 1, 3, 2), (3, 2, 1, 0), (2, 3, 0, 1), (1, 0, 2, 3)),
    (1, 1): ((2, 3, 0, 1), (0, 1, 2, 3), (3, 0, 1, 2), (1, 2, 3, 0)),
}


def back_z(n, z, core):
    return 2 * BACK[(z // 2) % 2, core][n][2 * (z // 4) + z % 2] + core


def to_tokens(n):
    return lambda x, y, z, core: (x, y, back_z(n, z, core), (z // 2) % 2)


def integers(index):
    x, y, z, core = place(index)
    row = slot_rows(x, y, z, core) + [core]
    for m in range(4):
        target = (z + shift(m, core, z % 2)) % 8
        row += [0 if (target // 2) % 2 == core else 1, target // 4]
    row.append(2 * (z % 2) + z // 4)
    source = {(z - shift(m, z % 2, core)) % 8: m for m in range(4)}
    row += [source[back_z(n, z, core)] for n in range(4)]
    row += slot_rows(x, y, z, 1 - core)
    for n in range(4):
        (origin,) = [
            a for a in range(8) if (a // 2) % 2 == core and back_z(n, a, z % 2) == z
        ]
        row.append(2 * (origin % 2) + origin // 4)
    return row


TABLE = np.array([integers(i) for i in range(256)], np.int32)


def nt(a, b):
    return lax.dot_general(a, b, (((1,), (1,)), ((), ())), preferred_element_type=F32)


def acts_kernel(own, other, out):
    for which, window in enumerate((own, other)):
        columns = window[...].T
        for odd in range(2):
            row = lax.broadcasted_iota(jnp.int32, (528, 384), 0)
            col = lax.broadcasted_iota(jnp.int32, (528, 384), 1)
            pick = jnp.where(row == 2 * col + odd, 1.0, 0.0).astype(BF16)
            picked = jnp.dot(columns, pick, preferred_element_type=F32)
            for step in range(3):
                lanes = slice(256 * which, 256 * which + 256)
                out[2 * step + odd, :, lanes] = picked[:, step : step + 256].astype(BF16)


def conv_kernel(base, table, acts, bias, *refs):
    *groups, out, weights, sems = refs
    groups = groups[-3:] if base == 0 else groups[-2:]
    copies = []
    at = 0
    for group in groups:
        for slot in range(group.shape[0]):
            for tap in range(5):
                copy = pltpu.make_async_copy(
                    group.at[slot, tap],
                    weights.at[at, :, pl.ds(768 * tap, 768)],
                    sems.at[at, tap],
                )
                copy.start()
                copies.append(copy)
            at += 1
    count = at
    shift = jnp.concatenate([bias[table[ROWS + base + i]] for i in range(count)], axis=0)
    for copy in copies:
        copy.wait()

    def block(number, _):
        cols = pl.ds(pl.multiple_of(256 * number, 256), 256)
        w = weights[...].reshape(48 * count, 3840)
        even = jnp.dot(w, acts[0:5, :, cols].reshape(3840, 256), preferred_element_type=F32)
        odd = jnp.dot(w, acts[1:6, :, cols].reshape(3840, 256), preferred_element_type=F32)
        pooled = (jnp.maximum(even, odd) + shift).astype(BF16)
        out[:, :, cols] = pooled.reshape(count, 48, 256)
        return 0

    lax.fori_loop(0, 2, block, 0)


def project_kernel(table, ma, mb, ta, tb, gain, g0, g1, g2, g3, g4, out, query, last, tokens, weights, normed, sems):
    at = 0
    copies = []
    for group in (g0, g1, g2, g3, g4):
        for slot in range(group.shape[0]):
            row = table[ROWS + at]
            for source, target in (
                (group.at[slot, pl.ds(0, 3)], weights.at[:, row % 2, row // 2]),
                (group.at[slot, 3], last.at[row]),
            ):
                copy = pltpu.make_async_copy(source, target, sems.at[len(copies)])
                copy.start()
                copies.append(copy)
            at += 1
    core = table[CORE]
    for at in range(16):
        a, b = (ma, at) if at < 12 else (mb, at - 12)
        tokens[core, table[ROWS + at]] = a[b]
        a = ta if at < 12 else tb
        row = table[OTHER + at]
        tokens[1 - core, row, :, :256] = a[b, :, 256:]
        tokens[1 - core, row, :, 256:] = a[b, :, :256]

    def norm(part, _):
        cols = pl.ds(pl.multiple_of(256 * part, 256), 256)
        values = [tokens[half, :, :, cols].astype(F32).reshape(768, 256) for half in range(2)]
        centre = sum(jnp.sum(v, axis=0, keepdims=True) for v in values) / 1536.0
        values = [v - centre for v in values]
        spread = sum(jnp.sum(v * v, axis=0, keepdims=True) for v in values) / 1536.0
        rate = lax.rsqrt(spread + 1e-05)
        for half in range(2):
            normed[part, half] = (values[half] * rate * gain[half]).astype(BF16)
        return 0

    lax.fori_loop(0, 2, norm, 0)
    for copy in copies:
        copy.wait()

    def one(m, _):
        part, head = table[SENDS + 2 * m], table[SENDS + 1 + 2 * m]
        total = None
        for half in range(2):
            w = weights[:, half, pl.ds(4 * head, 4)].reshape(576, 768)
            term = jnp.dot(w, normed[part, half], preferred_element_type=F32)
            total = term if total is None else total + term
        out[m] = total[:384].astype(BF16).reshape(2, 192, 256)
        query[m] = total[384:].astype(BF16)
        return 0

    lax.fori_loop(0, 4, one, 0)


def scores_of(query, groups, scores):
    top = None
    for at, group in enumerate(groups):
        keys = jnp.concatenate([group[i, 0] for i in range(group.shape[0])], axis=1)
        s = jnp.dot(query, keys, preferred_element_type=F32)
        scores[at, :, : s.shape[1]] = s
        t = jnp.max(s, axis=1, keepdims=True)
        top = t if top is None else jnp.maximum(top, t)
    return top


def sums_of(top, groups, scores, scale):
    top = top * scale
    total = acc = None
    for at, group in enumerate(groups):
        values = jnp.concatenate([group[i, 1] for i in range(group.shape[0])], axis=1)
        p = jnp.exp2(scores[at, :, : values.shape[1]] * scale - top)
        t = jnp.sum(p, axis=1, keepdims=True)
        o = nt(p.astype(BF16), values)
        total = t if total is None else total + t
        acc = o if acc is None else acc + o
    return total, acc


def attend_kernel(table, factor, queries, g0, g1, tops, totals, accs, scores):
    scale = factor[table[HEAD]] * (math.log2(math.e) / math.sqrt(HEAD_DIM))

    def one(part, _):
        groups = (g0, g1)
        top = scores_of(queries[part].T, groups, scores)
        total, acc = sums_of(top, groups, scores, scale)
        tops[part] = jnp.broadcast_to(top, (256, 128))
        totals[part] = jnp.broadcast_to(total, (256, 128))
        accs[part] = acc
        return 0

    lax.fori_loop(0, 4, one, 0)


def finish_kernel(table, factor, queries, g0, g1, tops, totals, accs, out, scores):
    scale = factor[table[HEAD]] * (math.log2(math.e) / math.sqrt(HEAD_DIM))

    def one(step, _):
        part = table[STEPS + step]
        groups = (g0, g1)
        before = tops[part, :, :1]
        top = jnp.maximum(before, scores_of(queries[part].T, groups, scores))
        total, acc = sums_of(top, groups, scores, scale)
        keep = jnp.exp2((before - top) * scale)
        total = total + totals[part, :, :1] * keep
        acc = acc + accs[part] * keep
        out[step] = (acc / total).astype(BF16).T
        return 0

    lax.fori_loop(0, 4, one, 0)


def base_kernel(tokens, out):
    for half in range(2):
        out[:, 768 * half : 768 * half + 768] = tokens[half, :, :, :256].reshape(768, 256).T


def out_kernel(table, h0, h1, h2, h3, base, mine, theirs, out, attended):
    core = table[CORE]
    for number, head in enumerate((h0, h1, h2, h3)):
        attended[table[FROM + number]] = head[...]
    rows = attended[...].reshape(768, 256).T
    for which, weights in ((core, mine), (1 - core, theirs)):
        lanes = pl.ds(pl.multiple_of(768 * which, 768), 768)
        mixed = nt(rows, weights[...].reshape(768, 768))
        out[:, lanes] = (base[:, lanes].astype(F32) + mixed).astype(BF16)


SMEM = pl.BlockSpec(memory_space=pltpu.SMEM)
VMEM = pl.BlockSpec(memory_space=pltpu.VMEM)
ANY = pl.BlockSpec(memory_space=pl.ANY)


def call(kernel, ins, outs, scratch, flops, *args):
    kernel_name = getattr(kernel, '__name__', 'kernel').replace('<lambda>', 'conv_kernel')
    return pl.pallas_call(
        kernel,
        out_shape=outs,
        in_specs=ins,
        out_specs=jax.tree.map(lambda _: VMEM, outs),
        scratch_shapes=scratch,
        compiler_params=pltpu.CompilerParams(vmem_limit_bytes=VMEM_BYTES),
        cost_estimate=pl.CostEstimate(flops=flops, bytes_accessed=BYTES, transcendentals=0),
        name=kernel_name,
    )(*args)


def shape(*dims, dtype=BF16):
    return jax.ShapeDtypeStruct(dims, dtype)


def shards(dna_features, conv_weight, conv_bias, norm_gain, qkv_weight, head_scale, out_weight):
    batch, seq = lax.axis_index("batch"), lax.axis_index("seq")
    core, high = batch % 2, (batch // 2) % 2
    table = lax.dynamic_index_in_dim(TABLE, batch * 16 + seq, 0, keepdims=False)

    taps = lax.dynamic_slice_in_dim(conv_weight.transpose(0, 2, 1), 48 * high, 48, axis=1)
    qkv = lax.dynamic_slice_in_dim(qkv_weight.transpose(0, 2, 1), 768 * high, 768, axis=2)
    last = lax.dynamic_slice_in_dim(out_weight.T, 48 * high, 48, axis=0)
    rest = jnp.concatenate([qkv[1:], qkv[:1], last[None]], axis=0)
    features = dna_features
    taps = send(taps, spread_z, "taps_z")
    rest = send(after(rest, taps), spread_z, "rest_z")

    activated = jax.nn.gelu(features.astype(F32), approximate=True).astype(BF16)
    forward = [(16 * b + i, 16 * b + i + 1) for b in range(16) for i in range(15)]
    backward = [(t, s) for s, t in forward]
    before = lax.ppermute(activated[-2:], AXES, forward)
    behind = lax.ppermute(activated[:2], AXES, backward)
    padded = jnp.concatenate([before, activated, behind, jnp.zeros((12, 768), BF16)], axis=0)
    acts = call(
        acts_kernel,
        [VMEM] * 2,
        shape(6, 768, 512),
        [],
        1_000_000_000,
        padded,
        send(padded, other_core, "acts_core"),
    )

    pieces = gather_first(taps, "taps_first")
    stack = stacked([after(pieces[0], rest)] + pieces[1:])
    pieces = gather_first(after(rest, *pieces[1:]), "rest_first")
    low, high_stack = [send(stack, second(step), "conv_second") for step in (1, -1)]
    onward = low[:2], high_stack[2:]
    far = send(onward[0], second(1), "conv_far"), send(onward[1], second(-1), "conv_far")
    qkv_stack = stacked([after(pieces[0], onward[1], acts)] + pieces[1:])
    qkv_near = [send(qkv_stack, second(step), "qkv_second") for step in (1, -1)]
    qkv_groups = (
        qkv_stack,
        *qkv_near,
        send(qkv_near[0][:2], second(1), "qkv_far"),
        send(qkv_near[1][2:], second(-1), "qkv_far"),
    )
    bias = lax.dynamic_slice_in_dim(conv_bias, 768 * core, 768).reshape(16, 48, 1)

    def conv(base, groups, *earlier):
        count = sum(g.shape[0] for g in groups)
        return call(
            lambda *refs: conv_kernel(base, *refs),
            [SMEM, VMEM, VMEM] + [ANY] * (len(groups) + len(earlier)),
            shape(count, 48, 512),
            [pltpu.VMEM((count, 48, 3840), BF16), pltpu.SemaphoreType.DMA((count, 5))],
            375_000_000 * count,
            table,
            acts,
            bias,
            *earlier,
            *groups,
        )

    mine = [conv(0, (stack, low, high_stack))]
    mine.append(conv(12, far, mine[0]))
    theirs = [send(m, other_core, "pooled_core") for m in mine]
    blocks, query, last, tokens = call(
        project_kernel,
        [SMEM] + [VMEM] * 5 + [ANY] * 5,
        [
            shape(4, 2, 192, 256),
            shape(4, 192, 256),
            shape(16, 48, 768),
            shape(2, 16, 48, 512),
        ],
        [
            pltpu.VMEM((3, 2, 8, 48, 768), BF16),
            pltpu.VMEM((2, 2, 768, 256), BF16),
            pltpu.SemaphoreType.DMA((32,)),
        ],
        1_800_000_000,
        table,
        *mine,
        *theirs,
        norm_gain.reshape(2, 768, 1),
        *qkv_groups,
    )

    keys = jnp.stack([send(blocks[m], to_head(m), "keys_z") for m in range(4)])
    far = send(keys, other_low, "keys_y")
    near = send(keys, other_core, "keys_core")
    query = after(query, keys)
    queries = jnp.stack([send(query[m], to_head(m), "queries_z") for m in range(4)])

    partial = call(
        attend_kernel,
        [SMEM, SMEM] + [VMEM] * 3,
        [
            shape(4, 256, 128, dtype=F32),
            shape(4, 256, 128, dtype=F32),
            shape(4, 256, 192, dtype=F32),
        ],
        [pltpu.VMEM((2, 256, 1024), F32)],
        1_600_000_000,
        table,
        head_scale,
        queries,
        keys,
        near,
    )
    base = call(base_kernel, [VMEM], shape(256, 1536), [], 1_000_000, tokens)
    other_last = send(after(last, queries), other_core, "out_core")
    far_near = send(far, other_core, "keys_y_core")
    heads = call(
        finish_kernel,
        [SMEM, SMEM] + [VMEM] * 6,
        shape(4, 192, 256),
        [pltpu.VMEM((2, 256, 1024), F32)],
        1_600_000_000,
        table,
        head_scale,
        queries,
        far,
        far_near,
        *partial,
    )
    back = [send(heads[n], to_tokens(n), "heads_back") for n in range(4)]
    return call(
        out_kernel,
        [SMEM] + [VMEM] * 7,
        shape(256, 1536),
        [pltpu.VMEM((4, 192, 256), BF16)],
        600_000_000,
        table,
        *back,
        base,
        last,
        other_last,
    )


def solution(mesh):
    placed = (
        P(AXES, None),
        P(None, None, "seq"),
        P(),
        P(),
        P(None, None, "seq"),
        P(),
        P(None, "seq"),
    )
    return jax.shard_map(
        shards, mesh=mesh, in_specs=placed, out_specs=P(AXES, None), check_vma=False
    )
```

```python
import math

import jax
import jax.numpy as jnp
import numpy as np
from jax import lax
from jax.experimental import pallas as pl
from jax.experimental.pallas import tpu as pltpu
from jax.sharding import PartitionSpec as P

HEADS = 4
HEAD_DIM = 192
AXES = ("batch", "seq")
F32 = jnp.float32
BF16 = jnp.bfloat16
DELTAS = (0, 1, -1, 2)
SLOTS = [(a, b) for b in range(4) for a in range(4)]
BYTES = 8_000_000
VMEM_BYTES = 60 * 1024 * 1024


def place(index):
    low, z = index % 2, (index // 2) % 8
    core, high, x = (index // 16) % 2, (index // 32) % 2, index // 64
    return x, 2 * high + low, z, core


def flat(x, y, z, core):
    x, y, z = x % 4, y % 4, z % 8
    return (((x * 2 + y // 2) * 2 + core) * 8 + z) * 2 + y % 2


def send(value, target, name):
    pairs = [(i, flat(*target(*place(i)))) for i in range(256)]
    with jax.named_scope(name):
        return lax.ppermute(value, AXES, pairs)


SPREAD = {
    (0, 0): ((3, 1, 0, 2), (0, 2, 1, 3), (2, 0, 3, 1), (1, 3, 2, 0)),
    (0, 1): ((2, 3, 0, 1), (0, 2, 1, 3), (3, 1, 2, 0), (1, 0, 3, 2)),
    (1, 0): ((1, 0, 3, 2), (0, 2, 1, 3), (3, 1, 2, 0), (2, 3, 0, 1)),
    (1, 1): ((2, 1, 3, 0), (0, 2, 1, 3), (3, 0, 2, 1), (1, 3, 0, 2)),
}


def origin_z(x, z, core):
    return SPREAD[core, z // 4][x % 4][z % 4]


def spread_z(x, y, z, core):
    (target,) = [i for i in range(4) if origin_z(x, 4 * core + i, z // 4) == z % 4]
    return x, y, 4 * core + target, z // 4


def first(step):
    return lambda x, y, z, core: (x + step, y, z, core) if core == 0 else (x, y + step, z, core)


def second(step):
    return lambda x, y, z, core: (x, y + step, z, core) if core == 0 else (x + step, y, z, core)


def other_core(x, y, z, core):
    return x, y, z, 1 - core


def other_low(x, y, z, core):
    return x, y ^ 1, z, core


def after(value, *others):
    zero = sum((o[(0,) * o.ndim].astype(F32) * 0.0 for o in others), F32(0.0))
    return value + zero.astype(value.dtype)


def stacked(blocks):
    out = jnp.zeros((len(blocks), *blocks[0].shape), blocks[0].dtype)
    for at in reversed(range(len(blocks))):
        out = lax.dynamic_update_slice(out, blocks[at][None], (at,) + (0,) * blocks[at].ndim)
    return out


def gather_first(block):
    return [block] + [send(block, first(step), "weights_first") for step in (1, -1, 2)]


ROWS, CORE, SENDS, HEAD, STEPS, OTHER, FROM = 0, 16, 17, 25, 26, 30, 46


def slot_rows(x, y, z, core):
    rows = []
    for a, b in SLOTS:
        along, across = (DELTAS[a], DELTAS[b]) if core == 0 else (DELTAS[b], DELTAS[a])
        px, py = (x - along) % 4, (y - across) % 4
        rows.append(origin_z(px, z, core) * 4 + (py % 2) * 2 + py // 2)
    return rows


def shift(m, core, parity):
    return (2, -2, 0, 4)[m] + core - parity


def to_head(m):
    return lambda x, y, z, core: (x, y, (z + shift(m, core, z % 2)) % 8, z % 2)


BACK = {
    (0, 0): ((1, 2, 3, 0), (3, 0, 1, 2), (0, 3, 2, 1), (2, 1, 0, 3)),
    (0, 1): ((2, 3, 0, 1), (0, 1, 2, 3), (1, 2, 3, 0), (3, 0, 1, 2)),
    (1, 0): ((0, 1, 3, 2), (3, 2, 1, 0), (2, 3, 0, 1), (1, 0, 2, 3)),
    (1, 1): ((2, 3, 0, 1), (0, 1, 2, 3), (3, 0, 1, 2), (1, 2, 3, 0)),
}


def back_z(n, z, core):
    return 2 * BACK[(z // 2) % 2, core][n][2 * (z // 4) + z % 2] + core


def to_tokens(n):
    return lambda x, y, z, core: (x, y, back_z(n, z, core), (z // 2) % 2)


def integers(index):
    x, y, z, core = place(index)
    row = slot_rows(x, y, z, core) + [core]
    for m in range(4):
        target = (z + shift(m, core, z % 2)) % 8
        row += [0 if (target // 2) % 2 == core else 1, target // 4]
    row.append(2 * (z % 2) + z // 4)
    source = {(z - shift(m, z % 2, core)) % 8: m for m in range(4)}
    row += [source[back_z(n, z, core)] for n in range(4)]
    row += slot_rows(x, y, z, 1 - core)
    for n in range(4):
        (origin,) = [
            a for a in range(8) if (a // 2) % 2 == core and back_z(n, a, z % 2) == z
        ]
        row.append(2 * (origin % 2) + origin // 4)
    return row


TABLE = np.array([integers(i) for i in range(256)], np.int32)


def nt(a, b):
    return lax.dot_general(a, b, (((1,), (1,)), ((), ())), preferred_element_type=F32)


def acts_kernel(own, other, out):
    for which, window in enumerate((own, other)):
        columns = window[...].T

        def one(number, _):
            row = lax.broadcasted_iota(jnp.int32, (528, 256), 0)
            col = lax.broadcasted_iota(jnp.int32, (528, 256), 1)
            pick = jnp.where(row == 2 * col + number, 1.0, 0.0).astype(BF16)
            picked = jnp.dot(columns, pick, preferred_element_type=F32)
            out[number, :, 256 * which : 256 * which + 256] = picked.astype(BF16)
            return 0

        lax.fori_loop(0, 6, one, 0)


def conv_kernel(base, table, acts, bias, *refs):
    *groups, out, weights, sems = refs
    groups = groups[-3:] if base == 0 else groups[-2:]
    copies = []
    at = 0
    for group in groups:
        for slot in range(group.shape[0]):
            for tap in range(5):
                copy = pltpu.make_async_copy(
                    group.at[slot, tap],
                    weights.at[at, :, pl.ds(768 * tap, 768)],
                    sems.at[at, tap],
                )
                copy.start()
                copies.append(copy)
            at += 1
    count = at
    shift = jnp.concatenate([bias[table[ROWS + base + i]] for i in range(count)], axis=0)
    for copy in copies:
        copy.wait()

    def block(number, _):
        cols = pl.ds(pl.multiple_of(256 * number, 256), 256)
        w = weights[...].reshape(48 * count, 3840)
        even = jnp.dot(w, acts[0:5, :, cols].reshape(3840, 256), preferred_element_type=F32)
        odd = jnp.dot(w, acts[1:6, :, cols].reshape(3840, 256), preferred_element_type=F32)
        pooled = (jnp.maximum(even, odd) + shift).astype(BF16)
        out[:, :, cols] = pooled.reshape(count, 48, 256)
        return 0

    lax.fori_loop(0, 2, block, 0)


def project_kernel(table, ma, mb, ta, tb, gain, g0, g1, g2, g3, g4, out, query, last, tokens, weights, normed, sems):
    at = 0
    copies = []
    for group in (g0, g1, g2, g3, g4):
        for slot in range(group.shape[0]):
            row = table[ROWS + at]
            for source, target in (
                (group.at[slot, pl.ds(0, 3)], weights.at[:, row % 2, row // 2]),
                (group.at[slot, 3], last.at[row]),
            ):
                copy = pltpu.make_async_copy(source, target, sems.at[len(copies)])
                copy.start()
                copies.append(copy)
            at += 1
    core = table[CORE]
    for at in range(16):
        a, b = (ma, at) if at < 12 else (mb, at - 12)
        tokens[core, table[ROWS + at]] = a[b]
        a = ta if at < 12 else tb
        row = table[OTHER + at]
        tokens[1 - core, row, :, :256] = a[b, :, 256:]
        tokens[1 - core, row, :, 256:] = a[b, :, :256]

    def norm(part, _):
        cols = pl.ds(pl.multiple_of(256 * part, 256), 256)
        values = [tokens[half, :, :, cols].astype(F32).reshape(768, 256) for half in range(2)]
        centre = sum(jnp.sum(v, axis=0, keepdims=True) for v in values) / 1536.0
        values = [v - centre for v in values]
        spread = sum(jnp.sum(v * v, axis=0, keepdims=True) for v in values) / 1536.0
        rate = lax.rsqrt(spread + 1e-05)
        for half in range(2):
            normed[part, half] = (values[half] * rate * gain[half]).astype(BF16)
        return 0

    lax.fori_loop(0, 2, norm, 0)
    for copy in copies:
        copy.wait()

    def one(m, _):
        part, head = table[SENDS + 2 * m], table[SENDS + 1 + 2 * m]
        total = None
        for half in range(2):
            w = weights[:, half, pl.ds(4 * head, 4)].reshape(576, 768)
            term = jnp.dot(w, normed[part, half], preferred_element_type=F32)
            total = term if total is None else total + term
        out[m] = total[:384].astype(BF16).reshape(2, 192, 256)
        query[m] = total[384:].astype(BF16)
        return 0

    lax.fori_loop(0, 4, one, 0)


def scores_of(query, groups, scores):
    top = None
    for at, group in enumerate(groups):
        keys = jnp.concatenate([group[i, 0] for i in range(group.shape[0])], axis=1)
        s = jnp.dot(query, keys, preferred_element_type=F32)
        scores[at, :, : s.shape[1]] = s
        t = jnp.max(s, axis=1, keepdims=True)
        top = t if top is None else jnp.maximum(top, t)
    return top


def sums_of(top, groups, scores, scale):
    top = top * scale
    total = acc = None
    for at, group in enumerate(groups):
        values = jnp.concatenate([group[i, 1] for i in range(group.shape[0])], axis=1)
        p = jnp.exp2(scores[at, :, : values.shape[1]] * scale - top)
        t = jnp.sum(p, axis=1, keepdims=True)
        o = nt(p.astype(BF16), values)
        total = t if total is None else total + t
        acc = o if acc is None else acc + o
    return total, acc


def attend_kernel(table, factor, queries, g0, g1, tops, totals, accs, scores):
    scale = factor[table[HEAD]] * (math.log2(math.e) / math.sqrt(HEAD_DIM))

    def one(part, _):
        groups = (g0, g1)
        top = scores_of(queries[part].T, groups, scores)
        total, acc = sums_of(top, groups, scores, scale)
        tops[part] = jnp.broadcast_to(top, (256, 128))
        totals[part] = jnp.broadcast_to(total, (256, 128))
        accs[part] = acc
        return 0

    lax.fori_loop(0, 4, one, 0)


def finish_kernel(table, factor, queries, g0, g1, tops, totals, accs, out, scores):
    scale = factor[table[HEAD]] * (math.log2(math.e) / math.sqrt(HEAD_DIM))

    def one(step, _):
        part = table[STEPS + step]
        groups = (g0, g1)
        before = tops[part, :, :1]
        top = jnp.maximum(before, scores_of(queries[part].T, groups, scores))
        total, acc = sums_of(top, groups, scores, scale)
        keep = jnp.exp2((before - top) * scale)
        total = total + totals[part, :, :1] * keep
        acc = acc + accs[part] * keep
        out[step] = (acc / total).astype(BF16).T
        return 0

    lax.fori_loop(0, 4, one, 0)


def base_kernel(tokens, out):
    for half in range(2):
        out[:, 768 * half : 768 * half + 768] = tokens[half, :, :, :256].reshape(768, 256).T


def out_kernel(table, h0, h1, h2, h3, base, mine, theirs, out, attended):
    core = table[CORE]
    for number, head in enumerate((h0, h1, h2, h3)):
        attended[table[FROM + number]] = head[...]
    rows = attended[...].reshape(768, 256).T
    for which, weights in ((core, mine), (1 - core, theirs)):
        lanes = pl.ds(pl.multiple_of(768 * which, 768), 768)
        mixed = nt(rows, weights[...].reshape(768, 768))
        out[:, lanes] = (base[:, lanes].astype(F32) + mixed).astype(BF16)


SMEM = pl.BlockSpec(memory_space=pltpu.SMEM)
VMEM = pl.BlockSpec(memory_space=pltpu.VMEM)
ANY = pl.BlockSpec(memory_space=pl.ANY)


def call(kernel, ins, outs, scratch, flops, *args):
    kernel_name = getattr(kernel, '__name__', 'kernel').replace('<lambda>', 'conv_kernel')
    return pl.pallas_call(
        kernel,
        out_shape=outs,
        in_specs=ins,
        out_specs=jax.tree.map(lambda _: VMEM, outs),
        scratch_shapes=scratch,
        compiler_params=pltpu.CompilerParams(vmem_limit_bytes=VMEM_BYTES),
        cost_estimate=pl.CostEstimate(flops=flops, bytes_accessed=BYTES, transcendentals=0),
        name=kernel_name,
    )(*args)


def shape(*dims, dtype=BF16):
    return jax.ShapeDtypeStruct(dims, dtype)


def shards(dna_features, conv_weight, conv_bias, norm_gain, qkv_weight, head_scale, out_weight):
    batch, seq = lax.axis_index("batch"), lax.axis_index("seq")
    core, high = batch % 2, (batch // 2) % 2
    table = lax.dynamic_index_in_dim(TABLE, batch * 16 + seq, 0, keepdims=False)

    taps = lax.dynamic_slice_in_dim(conv_weight.transpose(0, 2, 1), 48 * high, 48, axis=1)
    qkv = lax.dynamic_slice_in_dim(qkv_weight.transpose(0, 2, 1), 768 * high, 768, axis=2)
    last = lax.dynamic_slice_in_dim(out_weight.T, 48 * high, 48, axis=0)
    block = jnp.concatenate([taps, qkv[1:], qkv[:1], last[None]], axis=0)
    features = after(dna_features, block)
    block = send(block, spread_z, "weights_z")

    activated = jax.nn.gelu(features.astype(F32), approximate=True).astype(BF16)
    forward = [(16 * b + i, 16 * b + i + 1) for b in range(16) for i in range(15)]
    backward = [(t, s) for s, t in forward]
    before = lax.ppermute(activated[-2:], AXES, forward)
    behind = lax.ppermute(activated[:2], AXES, backward)
    padded = jnp.concatenate([before, activated, behind, jnp.zeros((12, 768), BF16)], axis=0)
    acts = call(
        acts_kernel,
        [VMEM] * 2,
        shape(6, 768, 512),
        [],
        1_000_000_000,
        padded,
        send(padded, other_core, "acts_core"),
    )

    pieces = gather_first(block)
    stack = stacked([after(pieces[0][:5], acts)] + [p[:5] for p in pieces[1:]])
    low, high_stack = [send(stack, second(step), "conv_second") for step in (1, -1)]
    far = (
        send(low[:2], second(1), "conv_far"),
        send(high_stack[2:], second(-1), "conv_far"),
    )
    qkv_stack = stacked([after(pieces[0][5:], high_stack)] + [p[5:] for p in pieces[1:]])
    qkv_near = [send(qkv_stack, second(step), "qkv_second") for step in (1, -1)]
    qkv_groups = (
        qkv_stack,
        *qkv_near,
        send(qkv_near[0][:2], second(1), "qkv_far"),
        send(qkv_near[1][2:], second(-1), "qkv_far"),
    )
    bias = lax.dynamic_slice_in_dim(conv_bias, 768 * core, 768).reshape(16, 48, 1)

    def conv(base, groups, *earlier):
        count = sum(g.shape[0] for g in groups)
        return call(
            lambda *refs: conv_kernel(base, *refs),
            [SMEM, VMEM, VMEM] + [ANY] * (len(groups) + len(earlier)),
            shape(count, 48, 512),
            [pltpu.VMEM((count, 48, 3840), BF16), pltpu.SemaphoreType.DMA((count, 5))],
            375_000_000 * count,
            table,
            acts,
            bias,
            *earlier,
            *groups,
        )

    mine = [conv(0, (stack, low, high_stack))]
    mine.append(conv(12, far, mine[0]))
    theirs = [send(m, other_core, "pooled_core") for m in mine]
    blocks, query, last, tokens = call(
        project_kernel,
        [SMEM] + [VMEM] * 5 + [ANY] * 5,
        [
            shape(4, 2, 192, 256),
            shape(4, 192, 256),
            shape(16, 48, 768),
            shape(2, 16, 48, 512),
        ],
        [
            pltpu.VMEM((3, 2, 8, 48, 768), BF16),
            pltpu.VMEM((2, 2, 768, 256), BF16),
            pltpu.SemaphoreType.DMA((32,)),
        ],
        1_800_000_000,
        table,
        *mine,
        *theirs,
        norm_gain.reshape(2, 768, 1),
        *qkv_groups,
    )

    keys = jnp.stack([send(blocks[m], to_head(m), "keys_z") for m in range(4)])
    far = send(keys, other_low, "keys_y")
    near = send(keys, other_core, "keys_core")
    query = after(query, keys)
    query = [send(query[m], to_head(m), "queries_z") for m in range(4)]
    queries = jnp.stack(query)

    partial = call(
        attend_kernel,
        [SMEM, SMEM] + [VMEM] * 3,
        [
            shape(4, 256, 128, dtype=F32),
            shape(4, 256, 128, dtype=F32),
            shape(4, 256, 192, dtype=F32),
        ],
        [pltpu.VMEM((2, 256, 1024), F32)],
        1_600_000_000,
        table,
        head_scale,
        queries,
        keys,
        near,
    )
    base = call(base_kernel, [VMEM], shape(256, 1536), [], 1_000_000, tokens)
    other_last = send(after(last, queries), other_core, "out_core")
    far_near = send(after(far, *query), other_core, "keys_y_core")
    heads = call(
        finish_kernel,
        [SMEM, SMEM] + [VMEM] * 6,
        shape(4, 192, 256),
        [pltpu.VMEM((2, 256, 1024), F32)],
        1_600_000_000,
        table,
        head_scale,
        queries,
        far,
        far_near,
        *partial,
    )
    back = [send(heads[n], to_tokens(n), "heads_back") for n in range(4)]
    return call(
        out_kernel,
        [SMEM] + [VMEM] * 7,
        shape(256, 1536),
        [pltpu.VMEM((4, 192, 256), BF16)],
        600_000_000,
        table,
        *back,
        base,
        last,
        other_last,
    )


def solution(mesh):
    placed = (
        P(AXES, None),
        P(None, None, "seq"),
        P(),
        P(),
        P(None, None, "seq"),
        P(),
        P(None, "seq"),
    )
    return jax.shard_map(
        shards, mesh=mesh, in_specs=placed, out_specs=P(AXES, None), check_vma=False
    )
```

```python
import math

import jax
import jax.numpy as jnp
import numpy as np
from jax import lax
from jax.experimental import pallas as pl
from jax.experimental.pallas import tpu as pltpu
from jax.sharding import PartitionSpec as P

HEADS = 4
HEAD_DIM = 192
AXES = ("batch", "seq")
F32 = jnp.float32
BF16 = jnp.bfloat16
DELTAS = (0, 1, -1, 2)
SLOTS = [(a, b) for b in range(4) for a in range(4)]
BYTES = 8_000_000
VMEM_BYTES = 60 * 1024 * 1024


def place(index):
    low, z = index % 2, (index // 2) % 8
    core, high, x = (index // 16) % 2, (index // 32) % 2, index // 64
    return x, 2 * high + low, z, core


def flat(x, y, z, core):
    x, y, z = x % 4, y % 4, z % 8
    return (((x * 2 + y // 2) * 2 + core) * 8 + z) * 2 + y % 2


def send(value, target, name):
    pairs = [(i, flat(*target(*place(i)))) for i in range(256)]
    with jax.named_scope(name):
        return lax.ppermute(value, AXES, pairs)


SPREAD = {
    (0, 0): ((3, 1, 0, 2), (0, 2, 1, 3), (2, 0, 3, 1), (1, 3, 2, 0)),
    (0, 1): ((2, 3, 0, 1), (0, 2, 1, 3), (3, 1, 2, 0), (1, 0, 3, 2)),
    (1, 0): ((1, 0, 3, 2), (0, 2, 1, 3), (3, 1, 2, 0), (2, 3, 0, 1)),
    (1, 1): ((2, 1, 3, 0), (0, 2, 1, 3), (3, 0, 2, 1), (1, 3, 0, 2)),
}


def origin_z(x, z, core):
    return SPREAD[core, z // 4][x % 4][z % 4]


def spread_z(x, y, z, core):
    (target,) = [i for i in range(4) if origin_z(x, 4 * core + i, z // 4) == z % 4]
    return x, y, 4 * core + target, z // 4


def first(step):
    return lambda x, y, z, core: (x + step, y, z, core) if core == 0 else (x, y + step, z, core)


def second(step):
    return lambda x, y, z, core: (x, y + step, z, core) if core == 0 else (x + step, y, z, core)


def other_core(x, y, z, core):
    return x, y, z, 1 - core


def other_low(x, y, z, core):
    return x, y ^ 1, z, core


def after(value, *others):
    zero = sum((o[(0,) * o.ndim].astype(F32) * 0.0 for o in others), F32(0.0))
    return value + zero.astype(value.dtype)


def stacked(blocks):
    out = jnp.zeros((len(blocks), *blocks[0].shape), blocks[0].dtype)
    for at in reversed(range(len(blocks))):
        out = lax.dynamic_update_slice(out, blocks[at][None], (at,) + (0,) * blocks[at].ndim)
    return out


def gather_first(block):
    return [block] + [send(block, first(step), "weights_first") for step in (1, -1, 2)]


ROWS, CORE, SENDS, HEAD, STEPS, OTHER, FROM = 0, 16, 17, 25, 26, 30, 46


def slot_rows(x, y, z, core):
    rows = []
    for a, b in SLOTS:
        along, across = (DELTAS[a], DELTAS[b]) if core == 0 else (DELTAS[b], DELTAS[a])
        px, py = (x - along) % 4, (y - across) % 4
        rows.append(origin_z(px, z, core) * 4 + (py % 2) * 2 + py // 2)
    return rows


def shift(m, core, parity):
    return (2, -2, 0, 4)[m] + core - parity


def to_head(m):
    return lambda x, y, z, core: (x, y, (z + shift(m, core, z % 2)) % 8, z % 2)


BACK = {
    (0, 0): ((1, 2, 3, 0), (3, 0, 1, 2), (0, 3, 2, 1), (2, 1, 0, 3)),
    (0, 1): ((2, 3, 0, 1), (0, 1, 2, 3), (1, 2, 3, 0), (3, 0, 1, 2)),
    (1, 0): ((0, 1, 3, 2), (3, 2, 1, 0), (2, 3, 0, 1), (1, 0, 2, 3)),
    (1, 1): ((2, 3, 0, 1), (0, 1, 2, 3), (3, 0, 1, 2), (1, 2, 3, 0)),
}


def back_z(n, z, core):
    return 2 * BACK[(z // 2) % 2, core][n][2 * (z // 4) + z % 2] + core


def to_tokens(n):
    return lambda x, y, z, core: (x, y, back_z(n, z, core), (z // 2) % 2)


def integers(index):
    x, y, z, core = place(index)
    row = slot_rows(x, y, z, core) + [core]
    for m in range(4):
        target = (z + shift(m, core, z % 2)) % 8
        row += [0 if (target // 2) % 2 == core else 1, target // 4]
    row.append(2 * (z % 2) + z // 4)
    source = {(z - shift(m, z % 2, core)) % 8: m for m in range(4)}
    row += [source[back_z(n, z, core)] for n in range(4)]
    row += slot_rows(x, y, z, 1 - core)
    for n in range(4):
        (origin,) = [
            a for a in range(8) if (a // 2) % 2 == core and back_z(n, a, z % 2) == z
        ]
        row.append(2 * (origin % 2) + origin // 4)
    return row


TABLE = np.array([integers(i) for i in range(256)], np.int32)


def nt(a, b):
    return lax.dot_general(a, b, (((1,), (1,)), ((), ())), preferred_element_type=F32)


def acts_kernel(own, other, out):
    for which, window in enumerate((own, other)):
        columns = window[...].T
        for odd in range(2):
            row = lax.broadcasted_iota(jnp.int32, (528, 384), 0)
            col = lax.broadcasted_iota(jnp.int32, (528, 384), 1)
            pick = jnp.where(row == 2 * col + odd, 1.0, 0.0).astype(BF16)
            picked = jnp.dot(columns, pick, preferred_element_type=F32)
            for step in range(3):
                lanes = slice(256 * which, 256 * which + 256)
                out[2 * step + odd, :, lanes] = picked[:, step : step + 256].astype(BF16)


def conv_kernel(base, table, acts, bias, *refs):
    *groups, out, weights, sems = refs
    groups = groups[-3:] if base == 0 else groups[-2:]
    copies = []
    at = 0
    for group in groups:
        for slot in range(group.shape[0]):
            for tap in range(5):
                copy = pltpu.make_async_copy(
                    group.at[slot, tap],
                    weights.at[at, :, pl.ds(768 * tap, 768)],
                    sems.at[at, tap],
                )
                copy.start()
                copies.append(copy)
            at += 1
    count = at
    shift = jnp.concatenate([bias[table[ROWS + base + i]] for i in range(count)], axis=0)
    for copy in copies:
        copy.wait()

    def block(number, _):
        cols = pl.ds(pl.multiple_of(256 * number, 256), 256)
        w = weights[...].reshape(48 * count, 3840)
        even = jnp.dot(w, acts[0:5, :, cols].reshape(3840, 256), preferred_element_type=F32)
        odd = jnp.dot(w, acts[1:6, :, cols].reshape(3840, 256), preferred_element_type=F32)
        pooled = (jnp.maximum(even, odd) + shift).astype(BF16)
        out[:, :, cols] = pooled.reshape(count, 48, 256)
        return 0

    lax.fori_loop(0, 2, block, 0)


def project_kernel(table, ma, mb, ta, tb, gain, g0, g1, g2, g3, g4, out, query, last, tokens, weights, normed, sems):
    at = 0
    copies = []
    for group in (g0, g1, g2, g3, g4):
        for slot in range(group.shape[0]):
            row = table[ROWS + at]
            for source, target in (
                (group.at[slot, pl.ds(0, 3)], weights.at[:, row % 2, row // 2]),
                (group.at[slot, 3], last.at[row]),
            ):
                copy = pltpu.make_async_copy(source, target, sems.at[len(copies)])
                copy.start()
                copies.append(copy)
            at += 1
    core = table[CORE]
    for at in range(16):
        a, b = (ma, at) if at < 12 else (mb, at - 12)
        tokens[core, table[ROWS + at]] = a[b]
        a = ta if at < 12 else tb
        row = table[OTHER + at]
        tokens[1 - core, row, :, :256] = a[b, :, 256:]
        tokens[1 - core, row, :, 256:] = a[b, :, :256]

    def norm(part, _):
        cols = pl.ds(pl.multiple_of(256 * part, 256), 256)
        values = [tokens[half, :, :, cols].astype(F32).reshape(768, 256) for half in range(2)]
        centre = sum(jnp.sum(v, axis=0, keepdims=True) for v in values) / 1536.0
        values = [v - centre for v in values]
        spread = sum(jnp.sum(v * v, axis=0, keepdims=True) for v in values) / 1536.0
        rate = lax.rsqrt(spread + 1e-05)
        for half in range(2):
            normed[part, half] = (values[half] * rate * gain[half]).astype(BF16)
        return 0

    lax.fori_loop(0, 2, norm, 0)
    for copy in copies:
        copy.wait()

    def one(m, _):
        part, head = table[SENDS + 2 * m], table[SENDS + 1 + 2 * m]
        total = None
        for half in range(2):
            w = weights[:, half, pl.ds(4 * head, 4)].reshape(576, 768)
            term = jnp.dot(w, normed[part, half], preferred_element_type=F32)
            total = term if total is None else total + term
        out[m] = total[:384].astype(BF16).reshape(2, 192, 256)
        query[m] = total[384:].astype(BF16)
        return 0

    lax.fori_loop(0, 4, one, 0)


def scores_of(query, groups, scores):
    top = None
    for at, group in enumerate(groups):
        keys = jnp.concatenate([group[i, 0] for i in range(group.shape[0])], axis=1)
        s = jnp.dot(query, keys, preferred_element_type=F32)
        scores[at, :, : s.shape[1]] = s
        t = jnp.max(s, axis=1, keepdims=True)
        top = t if top is None else jnp.maximum(top, t)
    return top


def sums_of(top, groups, scores, scale):
    top = top * scale
    total = acc = None
    for at, group in enumerate(groups):
        values = jnp.concatenate([group[i, 1] for i in range(group.shape[0])], axis=1)
        p = jnp.exp2(scores[at, :, : values.shape[1]] * scale - top)
        t = jnp.sum(p, axis=1, keepdims=True)
        o = nt(p.astype(BF16), values)
        total = t if total is None else total + t
        acc = o if acc is None else acc + o
    return total, acc


def attend_kernel(table, factor, queries, g0, g1, tops, totals, accs, scores):
    scale = factor[table[HEAD]] * (math.log2(math.e) / math.sqrt(HEAD_DIM))

    def one(part, _):
        groups = (g0, g1)
        top = scores_of(queries[part].T, groups, scores)
        total, acc = sums_of(top, groups, scores, scale)
        tops[part] = jnp.broadcast_to(top, (256, 128))
        totals[part] = jnp.broadcast_to(total, (256, 128))
        accs[part] = acc
        return 0

    lax.fori_loop(0, 4, one, 0)


def finish_kernel(table, factor, queries, g0, g1, tops, totals, accs, out, scores):
    scale = factor[table[HEAD]] * (math.log2(math.e) / math.sqrt(HEAD_DIM))

    def one(step, _):
        part = table[STEPS + step]
        groups = (g0, g1)
        before = tops[part, :, :1]
        top = jnp.maximum(before, scores_of(queries[part].T, groups, scores))
        total, acc = sums_of(top, groups, scores, scale)
        keep = jnp.exp2((before - top) * scale)
        total = total + totals[part, :, :1] * keep
        acc = acc + accs[part] * keep
        out[step] = (acc / total).astype(BF16).T
        return 0

    lax.fori_loop(0, 4, one, 0)


def base_kernel(tokens, out):
    for half in range(2):
        out[:, 768 * half : 768 * half + 768] = tokens[half, :, :, :256].reshape(768, 256).T


def out_kernel(table, h0, h1, h2, h3, base, mine, theirs, out, attended):
    core = table[CORE]
    for number, head in enumerate((h0, h1, h2, h3)):
        attended[table[FROM + number]] = head[...]
    rows = attended[...].reshape(768, 256).T
    for which, weights in ((core, mine), (1 - core, theirs)):
        lanes = pl.ds(pl.multiple_of(768 * which, 768), 768)
        mixed = nt(rows, weights[...].reshape(768, 768))
        out[:, lanes] = (base[:, lanes].astype(F32) + mixed).astype(BF16)


SMEM = pl.BlockSpec(memory_space=pltpu.SMEM)
VMEM = pl.BlockSpec(memory_space=pltpu.VMEM)
ANY = pl.BlockSpec(memory_space=pl.ANY)


def call(kernel, ins, outs, scratch, flops, *args):
    kernel_name = getattr(kernel, '__name__', 'kernel').replace('<lambda>', 'conv_kernel')
    return pl.pallas_call(
        kernel,
        out_shape=outs,
        in_specs=ins,
        out_specs=jax.tree.map(lambda _: VMEM, outs),
        scratch_shapes=scratch,
        compiler_params=pltpu.CompilerParams(vmem_limit_bytes=VMEM_BYTES),
        cost_estimate=pl.CostEstimate(flops=flops, bytes_accessed=BYTES, transcendentals=0),
        name=kernel_name,
    )(*args)


def shape(*dims, dtype=BF16):
    return jax.ShapeDtypeStruct(dims, dtype)


def shards(dna_features, conv_weight, conv_bias, norm_gain, qkv_weight, head_scale, out_weight):
    batch, seq = lax.axis_index("batch"), lax.axis_index("seq")
    core, high = batch % 2, (batch // 2) % 2
    table = lax.dynamic_index_in_dim(TABLE, batch * 16 + seq, 0, keepdims=False)

    taps = lax.dynamic_slice_in_dim(conv_weight.transpose(0, 2, 1), 48 * high, 48, axis=1)
    qkv = lax.dynamic_slice_in_dim(qkv_weight.transpose(0, 2, 1), 768 * high, 768, axis=2)
    last = lax.dynamic_slice_in_dim(out_weight.T, 48 * high, 48, axis=0)
    block = jnp.concatenate([taps, qkv[1:], qkv[:1], last[None]], axis=0)
    features = after(dna_features, block)
    block = send(block, spread_z, "weights_z")

    activated = jax.nn.gelu(features.astype(F32), approximate=True).astype(BF16)
    forward = [(16 * b + i, 16 * b + i + 1) for b in range(16) for i in range(15)]
    backward = [(t, s) for s, t in forward]
    before = lax.ppermute(activated[-2:], AXES, forward)
    behind = lax.ppermute(activated[:2], AXES, backward)
    padded = jnp.concatenate([before, activated, behind, jnp.zeros((12, 768), BF16)], axis=0)
    acts = call(
        acts_kernel,
        [VMEM] * 2,
        shape(6, 768, 512),
        [],
        1_000_000_000,
        padded,
        send(padded, other_core, "acts_core"),
    )

    pieces = gather_first(block)
    stack = stacked([after(pieces[0][:5], acts)] + [p[:5] for p in pieces[1:]])
    low, high_stack = [send(stack, second(step), "conv_second") for step in (1, -1)]
    far = (
        send(low[:2], second(1), "conv_far"),
        send(high_stack[2:], second(-1), "conv_far"),
    )
    qkv_stack = stacked([after(pieces[0][5:], high_stack)] + [p[5:] for p in pieces[1:]])
    qkv_near = [send(qkv_stack, second(step), "qkv_second") for step in (1, -1)]
    qkv_groups = (
        qkv_stack,
        *qkv_near,
        send(qkv_near[0][:2], second(1), "qkv_far"),
        send(qkv_near[1][2:], second(-1), "qkv_far"),
    )
    bias = lax.dynamic_slice_in_dim(conv_bias, 768 * core, 768).reshape(16, 48, 1)

    def conv(base, groups, *earlier):
        count = sum(g.shape[0] for g in groups)
        return call(
            lambda *refs: conv_kernel(base, *refs),
            [SMEM, VMEM, VMEM] + [ANY] * (len(groups) + len(earlier)),
            shape(count, 48, 512),
            [pltpu.VMEM((count, 48, 3840), BF16), pltpu.SemaphoreType.DMA((count, 5))],
            375_000_000 * count,
            table,
            acts,
            bias,
            *earlier,
            *groups,
        )

    mine = [conv(0, (stack, low, high_stack))]
    mine.append(conv(12, far, mine[0]))
    theirs = [send(m, other_core, "pooled_core") for m in mine]
    blocks, query, last, tokens = call(
        project_kernel,
        [SMEM] + [VMEM] * 5 + [ANY] * 5,
        [
            shape(4, 2, 192, 256),
            shape(4, 192, 256),
            shape(16, 48, 768),
            shape(2, 16, 48, 512),
        ],
        [
            pltpu.VMEM((3, 2, 8, 48, 768), BF16),
            pltpu.VMEM((2, 2, 768, 256), BF16),
            pltpu.SemaphoreType.DMA((32,)),
        ],
        1_800_000_000,
        table,
        *mine,
        *theirs,
        norm_gain.reshape(2, 768, 1),
        *qkv_groups,
    )

    keys = jnp.stack([send(blocks[m], to_head(m), "keys_z") for m in range(4)])
    far = send(keys, other_low, "keys_y")
    near = send(keys, other_core, "keys_core")
    query = after(query, keys)
    query = [send(query[m], to_head(m), "queries_z") for m in range(4)]
    queries = jnp.stack(query)

    partial = call(
        attend_kernel,
        [SMEM, SMEM] + [VMEM] * 3,
        [
            shape(4, 256, 128, dtype=F32),
            shape(4, 256, 128, dtype=F32),
            shape(4, 256, 192, dtype=F32),
        ],
        [pltpu.VMEM((2, 256, 1024), F32)],
        1_600_000_000,
        table,
        head_scale,
        queries,
        keys,
        near,
    )
    base = call(base_kernel, [VMEM], shape(256, 1536), [], 1_000_000, tokens)
    other_last = send(after(last, queries), other_core, "out_core")
    far_near = send(after(far, *query), other_core, "keys_y_core")
    heads = call(
        finish_kernel,
        [SMEM, SMEM] + [VMEM] * 6,
        shape(4, 192, 256),
        [pltpu.VMEM((2, 256, 1024), F32)],
        1_600_000_000,
        table,
        head_scale,
        queries,
        far,
        far_near,
        *partial,
    )
    back = [send(heads[n], to_tokens(n), "heads_back") for n in range(4)]
    return call(
        out_kernel,
        [SMEM] + [VMEM] * 7,
        shape(256, 1536),
        [pltpu.VMEM((4, 192, 256), BF16)],
        600_000_000,
        table,
        *back,
        base,
        last,
        other_last,
    )


def solution(mesh):
    placed = (
        P(AXES, None),
        P(None, None, "seq"),
        P(),
        P(),
        P(None, None, "seq"),
        P(),
        P(None, "seq"),
    )
    return jax.shard_map(
        shards, mesh=mesh, in_specs=placed, out_specs=P(AXES, None), check_vma=False
    )
```

```python
import math

import jax
import jax.numpy as jnp
import numpy as np
from jax import lax
from jax.experimental import pallas as pl
from jax.experimental.pallas import tpu as pltpu
from jax.sharding import PartitionSpec as P

HEADS = 4
HEAD_DIM = 192
AXES = ("batch", "seq")
F32 = jnp.float32
BF16 = jnp.bfloat16
DELTAS = (0, 1, -1, 2)
SLOTS = [(a, b) for b in range(4) for a in range(4)]
BYTES = 8_000_000
VMEM_BYTES = 60 * 1024 * 1024


def place(index):
    low, z = index % 2, (index // 2) % 8
    core, high, x = (index // 16) % 2, (index // 32) % 2, index // 64
    return x, 2 * high + low, z, core


def flat(x, y, z, core):
    x, y, z = x % 4, y % 4, z % 8
    return (((x * 2 + y // 2) * 2 + core) * 8 + z) * 2 + y % 2


def send(value, target, name):
    pairs = [(i, flat(*target(*place(i)))) for i in range(256)]
    with jax.named_scope(name):
        return lax.ppermute(value, AXES, pairs)


SPREAD = {
    (0, 0): ((3, 1, 0, 2), (0, 2, 1, 3), (2, 0, 3, 1), (1, 3, 2, 0)),
    (0, 1): ((2, 3, 0, 1), (0, 2, 1, 3), (3, 1, 2, 0), (1, 0, 3, 2)),
    (1, 0): ((1, 0, 3, 2), (0, 2, 1, 3), (3, 1, 2, 0), (2, 3, 0, 1)),
    (1, 1): ((2, 1, 3, 0), (0, 2, 1, 3), (3, 0, 2, 1), (1, 3, 0, 2)),
}


def origin_z(x, z, core):
    return SPREAD[core, z // 4][x % 4][z % 4]


def spread_z(x, y, z, core):
    (target,) = [i for i in range(4) if origin_z(x, 4 * core + i, z // 4) == z % 4]
    return x, y, 4 * core + target, z // 4


def first(step):
    return lambda x, y, z, core: (x + step, y, z, core) if core == 0 else (x, y + step, z, core)


def second(step):
    return lambda x, y, z, core: (x, y + step, z, core) if core == 0 else (x + step, y, z, core)


def other_core(x, y, z, core):
    return x, y, z, 1 - core


def other_low(x, y, z, core):
    return x, y ^ 1, z, core


def after(value, *others):
    zero = sum((o[(0,) * o.ndim].astype(F32) * 0.0 for o in others), F32(0.0))
    return value + zero.astype(value.dtype)


def stacked(blocks):
    out = jnp.zeros((len(blocks), *blocks[0].shape), blocks[0].dtype)
    for at in reversed(range(len(blocks))):
        out = lax.dynamic_update_slice(out, blocks[at][None], (at,) + (0,) * blocks[at].ndim)
    return out


def gather_first(block):
    return [block] + [send(block, first(step), "weights_first") for step in (1, -1, 2)]


ROWS, CORE, SENDS, HEAD, STEPS, OTHER, FROM = 0, 16, 17, 25, 26, 30, 46


def slot_rows(x, y, z, core):
    rows = []
    for a, b in SLOTS:
        along, across = (DELTAS[a], DELTAS[b]) if core == 0 else (DELTAS[b], DELTAS[a])
        px, py = (x - along) % 4, (y - across) % 4
        rows.append(origin_z(px, z, core) * 4 + (py % 2) * 2 + py // 2)
    return rows


def shift(m, core, parity):
    return (2, -2, 0, 4)[m] + core - parity


def to_head(m):
    return lambda x, y, z, core: (x, y, (z + shift(m, core, z % 2)) % 8, z % 2)


BACK = {
    (0, 0): ((1, 2, 3, 0), (3, 0, 1, 2), (0, 3, 2, 1), (2, 1, 0, 3)),
    (0, 1): ((2, 3, 0, 1), (0, 1, 2, 3), (1, 2, 3, 0), (3, 0, 1, 2)),
    (1, 0): ((0, 1, 3, 2), (3, 2, 1, 0), (2, 3, 0, 1), (1, 0, 2, 3)),
    (1, 1): ((2, 3, 0, 1), (0, 1, 2, 3), (3, 0, 1, 2), (1, 2, 3, 0)),
}


def back_z(n, z, core):
    return 2 * BACK[(z // 2) % 2, core][n][2 * (z // 4) + z % 2] + core


def to_tokens(n):
    return lambda x, y, z, core: (x, y, back_z(n, z, core), (z // 2) % 2)


def integers(index):
    x, y, z, core = place(index)
    row = slot_rows(x, y, z, core) + [core]
    for m in range(4):
        target = (z + shift(m, core, z % 2)) % 8
        row += [0 if (target // 2) % 2 == core else 1, target // 4]
    row.append(2 * (z % 2) + z // 4)
    source = {(z - shift(m, z % 2, core)) % 8: m for m in range(4)}
    row += [source[back_z(n, z, core)] for n in range(4)]
    row += slot_rows(x, y, z, 1 - core)
    for n in range(4):
        (origin,) = [
            a for a in range(8) if (a // 2) % 2 == core and back_z(n, a, z % 2) == z
        ]
        row.append(2 * (origin % 2) + origin // 4)
    return row


TABLE = np.array([integers(i) for i in range(256)], np.int32)


def column(row):
    return jnp.broadcast_to(row, (8, row.shape[1])).T[:, :1]


def nt(a, b):
    return lax.dot_general(a, b, (((1,), (1,)), ((), ())), preferred_element_type=F32)


def acts_kernel(own, other, out):
    for which, window in enumerate((own, other)):
        columns = window[...].T
        for odd in range(2):
            row = lax.broadcasted_iota(jnp.int32, (528, 384), 0)
            col = lax.broadcasted_iota(jnp.int32, (528, 384), 1)
            pick = jnp.where(row == 2 * col + odd, 1.0, 0.0).astype(BF16)
            picked = jnp.dot(columns, pick, preferred_element_type=F32)
            for step in range(3):
                lanes = slice(256 * which, 256 * which + 256)
                out[2 * step + odd, :, lanes] = picked[:, step : step + 256].astype(BF16)


def conv_kernel(base, table, acts, bias, *refs):
    *groups, out, weights, sems = refs
    groups = groups[-3:] if base == 0 else groups[-2:]
    copies = []
    at = 0
    for group in groups:
        for slot in range(group.shape[0]):
            for tap in range(5):
                copy = pltpu.make_async_copy(
                    group.at[slot, tap],
                    weights.at[at, :, pl.ds(768 * tap, 768)],
                    sems.at[at, tap],
                )
                copy.start()
                copies.append(copy)
            at += 1
    count = at
    shift = jnp.concatenate([bias[table[ROWS + base + i]] for i in range(count)], axis=0)
    for copy in copies:
        copy.wait()

    def block(number, _):
        cols = pl.ds(pl.multiple_of(256 * number, 256), 256)
        w = weights[...].reshape(48 * count, 3840)
        even = jnp.dot(w, acts[0:5, :, cols].reshape(3840, 256), preferred_element_type=F32)
        odd = jnp.dot(w, acts[1:6, :, cols].reshape(3840, 256), preferred_element_type=F32)
        pooled = (jnp.maximum(even, odd) + shift).astype(BF16)
        out[:, :, cols] = pooled.reshape(count, 48, 256)
        return 0

    lax.fori_loop(0, 2, block, 0)


def project_kernel(table, ma, mb, ta, tb, gain, g0, g1, g2, g3, g4, out, query, last, tokens, weights, normed, sems):
    at = 0
    copies = []
    for group in (g0, g1, g2, g3, g4):
        for slot in range(group.shape[0]):
            row = table[ROWS + at]
            for source, target in (
                (group.at[slot, pl.ds(0, 3)], weights.at[:, row % 2, row // 2]),
                (group.at[slot, 3], last.at[row]),
            ):
                copy = pltpu.make_async_copy(source, target, sems.at[len(copies)])
                copy.start()
                copies.append(copy)
            at += 1
    core = table[CORE]
    for at in range(16):
        a, b = (ma, at) if at < 12 else (mb, at - 12)
        tokens[core, table[ROWS + at]] = a[b]
        a = ta if at < 12 else tb
        row = table[OTHER + at]
        tokens[1 - core, row, :, :256] = a[b, :, 256:]
        tokens[1 - core, row, :, 256:] = a[b, :, :256]

    def norm(part, _):
        cols = pl.ds(pl.multiple_of(256 * part, 256), 256)
        values = [tokens[half, :, :, cols].astype(F32).reshape(768, 256) for half in range(2)]
        centre = sum(jnp.sum(v, axis=0, keepdims=True) for v in values) / 1536.0
        values = [v - centre for v in values]
        spread = sum(jnp.sum(v * v, axis=0, keepdims=True) for v in values) / 1536.0
        rate = lax.rsqrt(spread + 1e-05)
        for half in range(2):
            normed[part, half] = (values[half] * rate * column(gain[half])).astype(BF16)
        return 0

    lax.fori_loop(0, 2, norm, 0)
    for copy in copies:
        copy.wait()

    def one(m, _):
        part, head = table[SENDS + 2 * m], table[SENDS + 1 + 2 * m]
        total = None
        for half in range(2):
            w = weights[:, half, pl.ds(4 * head, 4)].reshape(576, 768)
            term = jnp.dot(w, normed[part, half], preferred_element_type=F32)
            total = term if total is None else total + term
        out[m] = total[:384].astype(BF16).reshape(2, 192, 256)
        query[m] = total[384:].astype(BF16)
        return 0

    lax.fori_loop(0, 4, one, 0)


def scores_of(query, groups, scores):
    top = None
    for at, group in enumerate(groups):
        keys = jnp.concatenate([group[i, 0] for i in range(group.shape[0])], axis=1)
        s = jnp.dot(query, keys, preferred_element_type=F32)
        scores[at, :, : s.shape[1]] = s
        t = jnp.max(s, axis=1, keepdims=True)
        top = t if top is None else jnp.maximum(top, t)
    return top


def sums_of(top, groups, scores, scale):
    top = top * scale
    total = acc = None
    for at, group in enumerate(groups):
        values = jnp.concatenate([group[i, 1] for i in range(group.shape[0])], axis=1)
        p = jnp.exp2(scores[at, :, : values.shape[1]] * scale - top)
        t = jnp.sum(p, axis=1, keepdims=True)
        o = nt(p.astype(BF16), values)
        total = t if total is None else total + t
        acc = o if acc is None else acc + o
    return total, acc


def attend_kernel(table, factor, queries, g0, g1, tops, totals, accs, scores):
    scale = factor[table[HEAD]] * (math.log2(math.e) / math.sqrt(HEAD_DIM))

    def one(part, _):
        groups = (g0, g1)
        top = scores_of(queries[part].T, groups, scores)
        total, acc = sums_of(top, groups, scores, scale)
        tops[part] = jnp.broadcast_to(top, (256, 128))
        totals[part] = jnp.broadcast_to(total, (256, 128))
        accs[part] = acc
        return 0

    lax.fori_loop(0, 4, one, 0)


def finish_kernel(table, factor, queries, g0, g1, tops, totals, accs, out, scores):
    scale = factor[table[HEAD]] * (math.log2(math.e) / math.sqrt(HEAD_DIM))

    def one(step, _):
        part = table[STEPS + step]
        groups = (g0, g1)
        before = tops[part, :, :1]
        top = jnp.maximum(before, scores_of(queries[part].T, groups, scores))
        total, acc = sums_of(top, groups, scores, scale)
        keep = jnp.exp2((before - top) * scale)
        total = total + totals[part, :, :1] * keep
        acc = acc + accs[part] * keep
        out[step] = (acc / total).astype(BF16).T
        return 0

    lax.fori_loop(0, 4, one, 0)


def base_kernel(tokens, out):
    for half in range(2):
        out[:, 768 * half : 768 * half + 768] = tokens[half, :, :, :256].reshape(768, 256).T


def out_kernel(table, h0, h1, h2, h3, base, mine, theirs, out, attended):
    core = table[CORE]
    for number, head in enumerate((h0, h1, h2, h3)):
        attended[table[FROM + number]] = head[...]
    rows = attended[...].reshape(768, 256).T
    for which, weights in ((core, mine), (1 - core, theirs)):
        lanes = pl.ds(pl.multiple_of(768 * which, 768), 768)
        mixed = nt(rows, weights[...].reshape(768, 768))
        out[:, lanes] = (base[:, lanes].astype(F32) + mixed).astype(BF16)


SMEM = pl.BlockSpec(memory_space=pltpu.SMEM)
VMEM = pl.BlockSpec(memory_space=pltpu.VMEM)
ANY = pl.BlockSpec(memory_space=pl.ANY)


def call(kernel, ins, outs, scratch, flops, *args):
    kernel_name = getattr(kernel, '__name__', 'kernel').replace('<lambda>', 'conv_kernel')
    return pl.pallas_call(
        kernel,
        out_shape=outs,
        in_specs=ins,
        out_specs=jax.tree.map(lambda _: VMEM, outs),
        scratch_shapes=scratch,
        compiler_params=pltpu.CompilerParams(vmem_limit_bytes=VMEM_BYTES),
        cost_estimate=pl.CostEstimate(flops=flops, bytes_accessed=BYTES, transcendentals=0),
        name=kernel_name,
    )(*args)


def shape(*dims, dtype=BF16):
    return jax.ShapeDtypeStruct(dims, dtype)


def shards(dna_features, conv_weight, conv_bias, norm_gain, qkv_weight, head_scale, out_weight):
    batch, seq = lax.axis_index("batch"), lax.axis_index("seq")
    core, high = batch % 2, (batch // 2) % 2
    table = lax.dynamic_index_in_dim(TABLE, batch * 16 + seq, 0, keepdims=False)

    taps = lax.dynamic_slice_in_dim(conv_weight.transpose(0, 2, 1), 48 * high, 48, axis=1)
    qkv = lax.dynamic_slice_in_dim(qkv_weight.transpose(0, 2, 1), 768 * high, 768, axis=2)
    last = lax.dynamic_slice_in_dim(out_weight.T, 48 * high, 48, axis=0)
    block = jnp.concatenate([taps, qkv[1:], qkv[:1], last[None]], axis=0)
    features = after(dna_features, block)
    block = send(block, spread_z, "weights_z")

    activated = jax.nn.gelu(features.astype(F32), approximate=True).astype(BF16)
    forward = [(16 * b + i, 16 * b + i + 1) for b in range(16) for i in range(15)]
    backward = [(t, s) for s, t in forward]
    before = lax.ppermute(activated[-2:], AXES, forward)
    behind = lax.ppermute(activated[:2], AXES, backward)
    padded = jnp.concatenate([before, activated, behind, jnp.zeros((12, 768), BF16)], axis=0)
    acts = call(
        acts_kernel,
        [VMEM] * 2,
        shape(6, 768, 512),
        [],
        1_000_000_000,
        padded,
        send(padded, other_core, "acts_core"),
    )

    pieces = gather_first(block)
    stack = stacked([after(pieces[0][:5], acts)] + [p[:5] for p in pieces[1:]])
    low, high_stack = [send(stack, second(step), "conv_second") for step in (1, -1)]
    far = (
        send(low[:2], second(1), "conv_far"),
        send(high_stack[2:], second(-1), "conv_far"),
    )
    qkv_stack = stacked([after(pieces[0][5:], high_stack)] + [p[5:] for p in pieces[1:]])
    qkv_near = [send(qkv_stack, second(step), "qkv_second") for step in (1, -1)]
    qkv_groups = (
        qkv_stack,
        *qkv_near,
        send(qkv_near[0][:2], second(1), "qkv_far"),
        send(qkv_near[1][2:], second(-1), "qkv_far"),
    )
    bias = lax.dynamic_slice_in_dim(conv_bias, 768 * core, 768).reshape(16, 48, 1)

    def conv(base, groups, *earlier):
        count = sum(g.shape[0] for g in groups)
        return call(
            lambda *refs: conv_kernel(base, *refs),
            [SMEM, VMEM, VMEM] + [ANY] * (len(groups) + len(earlier)),
            shape(count, 48, 512),
            [pltpu.VMEM((count, 48, 3840), BF16), pltpu.SemaphoreType.DMA((count, 5))],
            375_000_000 * count,
            table,
            acts,
            bias,
            *earlier,
            *groups,
        )

    mine = [conv(0, (stack, low, high_stack))]
    mine.append(conv(12, far, mine[0]))
    theirs = [send(m, other_core, "pooled_core") for m in mine]
    blocks, query, last, tokens = call(
        project_kernel,
        [SMEM] + [VMEM] * 5 + [ANY] * 5,
        [
            shape(4, 2, 192, 256),
            shape(4, 192, 256),
            shape(16, 48, 768),
            shape(2, 16, 48, 512),
        ],
        [
            pltpu.VMEM((3, 2, 8, 48, 768), BF16),
            pltpu.VMEM((2, 2, 768, 256), BF16),
            pltpu.SemaphoreType.DMA((32,)),
        ],
        1_800_000_000,
        table,
        *mine,
        *theirs,
        norm_gain.reshape(2, 1, 768),
        *qkv_groups,
    )

    keys = jnp.stack([send(blocks[m], to_head(m), "keys_z") for m in range(4)])
    far = send(keys, other_low, "keys_y")
    near = send(keys, other_core, "keys_core")
    query = after(query, keys)
    query = [send(query[m], to_head(m), "queries_z") for m in range(4)]
    queries = jnp.stack(query)

    partial = call(
        attend_kernel,
        [SMEM, SMEM] + [VMEM] * 3,
        [
            shape(4, 256, 128, dtype=F32),
            shape(4, 256, 128, dtype=F32),
            shape(4, 256, 192, dtype=F32),
        ],
        [pltpu.VMEM((2, 256, 1024), F32)],
        1_600_000_000,
        table,
        head_scale,
        queries,
        keys,
        near,
    )
    base = call(base_kernel, [VMEM], shape(256, 1536), [], 1_000_000, tokens)
    other_last = send(after(last, queries), other_core, "out_core")
    far_near = send(after(far, *query), other_core, "keys_y_core")
    heads = call(
        finish_kernel,
        [SMEM, SMEM] + [VMEM] * 6,
        shape(4, 192, 256),
        [pltpu.VMEM((2, 256, 1024), F32)],
        1_600_000_000,
        table,
        head_scale,
        queries,
        far,
        far_near,
        *partial,
    )
    back = [send(heads[n], to_tokens(n), "heads_back") for n in range(4)]
    return call(
        out_kernel,
        [SMEM] + [VMEM] * 7,
        shape(256, 1536),
        [pltpu.VMEM((4, 192, 256), BF16)],
        600_000_000,
        table,
        *back,
        base,
        last,
        other_last,
    )


def solution(mesh):
    placed = (
        P(AXES, None),
        P(None, None, "seq"),
        P(),
        P(),
        P(None, None, "seq"),
        P(),
        P(None, "seq"),
    )
    return jax.shard_map(
        shards, mesh=mesh, in_specs=placed, out_specs=P(AXES, None), check_vma=False
    )
```
